256 devices in a mesh: dp: 4 (over y), expert: 64 (over x, z, core).
Axes of the slice: x: 4, y: 4, z: 8, core: 2. Of those that a mesh axis runs over, the one named last changes fastest.
Arguments:
- tokens: bfloat16 [32768, 2048], P(('dp', 'expert')), may hold values from -6 to 6
- expert_ids: int32 [32768, 3], P(('dp', 'expert')), may hold values from 0 to 63, all different within a row; in each aligned block of 128 rows (0 to 127, 128 to 255, ...) at most 8 rows name the same one
- gate_level: int32 [32768, 3], P(('dp', 'expert')), may hold values from 0 to 15
- cost_bucket: int32 [512], P(('dp', 'expert')), may hold values from 0 to 7
- gate_table: float32 [8, 16], replicated, may hold values from 0.05 to 0.6
- gate_weight: bfloat16 [64, 2048, 768], P('expert', 'dp'), may hold values from -0.125 to 0.125
- up_weight: bfloat16 [64, 2048, 768], P('expert', 'dp'), may hold values from -0.125 to 0.125
- down_weight: bfloat16 [64, 2048, 768], P('expert', 'dp'), may hold values from -0.21875 to 0.21875
- out_grad: bfloat16 [32768, 2048], P(('dp', 'expert')), may hold values from -6 to 6
Outputs:
- output: bfloat16 [32768, 2048], P(('dp', 'expert'))
- token_grad: bfloat16 [32768, 2048], P(('dp', 'expert'))
- gate_grad: float32 [64, 2048, 768], P('expert', 'dp')
- up_grad: float32 [64, 2048, 768], P('expert', 'dp')
- down_grad: float32 [64, 2048, 768], P('expert', 'dp')
The draws below stay inside these ranges and needn't reach their ends.
Inputs may be any that keep to these rules, and one draw needn't show every extreme that they name: `expert_ids`: each row names 3 different experts. Among the rows of one device (aligned blocks of 128 rows) no expert is named more than 8 times, and in every draw some expert is named exactly 8 times in some block.
All inputs are finite; a program needn't handle non-finite values.
Results may differ from the reference program's by a relative error of at most 0.0085.
Values may be sent and summed in bfloat16 or wider, within the bound.
No kernel may reach another device: no remote copies, remote signals or barrier semaphores. Data moves between devices by JAX's collectives and lax.ppermute only.
A program may use at most 128 MiB of HBM per device.

```python
import math
import jax
import jax.numpy as jnp
import numpy as np
from jax import lax

D = 2048
H = 768
TOP = 3
TOK_DEV = 128
TRAJ = 64
BUCKETS = 8
LEVELS = 16
EXPERTS = 64
CAP = 8
TOKENS = 32768
TRAJS = 512
N_DP = 4


def set_ends(array, rng, smallest, largest):
    longest = array.shape.index(max(array.shape))
    spots = []
    for shift in (0, 1):
        where = [jax.random.randint(jax.random.fold_in(rng, axis), (), 0, length) for axis, length in enumerate(array.shape)]
        where[longest] = (where[longest] + shift) % array.shape[longest]
        spots.append(tuple(where))
    return array.at[spots[0]].set(smallest).at[spots[1]].set(largest)


def block_levels(stream_key, dims, split, smallest, largest):
    loudness = 1.0
    for dim, blocks in split:
        heights = jax.random.uniform(jax.random.fold_in(jax.random.fold_in(stream_key, 6), dim), (blocks,), jnp.float32, smallest / len(split), largest / len(split))
        loudness = loudness * jnp.repeat(jnp.exp(heights), dims[dim] // blocks).reshape((-1,) + (1,) * (len(dims) - 1 - dim))
    return loudness


def deal_out(own_key, own, number, rows, number_of, top, most, slope):
    ranking = jax.random.permutation(own_key, number_of)
    heavy_load, usual = load_shares(number_of, rows * top, most, slope, True), load_shares(number_of, rows * top, most, slope, False)
    places = jnp.arange(number_of)

    def named(lengths, turn):
        used = int((lengths > 0).sum())
        fixed = max(1, used // 4)
        shifted = fixed + (places - fixed + turn * (used - fixed)) % max(1, number_of - fixed)
        return jnp.zeros((number_of,), jnp.int32).at[ranking[jnp.where(places < fixed, places, shifted)]].set(jnp.asarray(lengths, jnp.int32))

    lengths = jnp.where(number % 4 == 0, named(heavy_load, number // 4), named(usual, number - number // 4 - 1))
    mixed = jax.random.permutation(jax.random.fold_in(own, 3), number_of)
    source_of, taker = mixed[0:number_of // 2 * 2:2], mixed[1:number_of // 2 * 2:2]
    room = jnp.minimum(lengths[source_of] - 1, most - lengths[taker]) // 2
    room = jnp.where((source_of == ranking[0]) | (taker == ranking[0]) | (lengths[taker] == 0), 0, jnp.maximum(room, 0))
    shifted = jax.random.randint(jax.random.fold_in(own, 4), (number_of // 2,), 0, 1 << 20) % (room + 1)
    lengths = lengths.at[source_of].add(-shifted).at[taker].add(shifted)
    items = jnp.searchsorted(jnp.cumsum(lengths), jnp.arange(rows * top), side="right").astype(jnp.int32)
    listing = items.reshape(top, rows).T
    listing = listing[jax.random.permutation(jax.random.fold_in(own, 1), rows)]
    turn = jax.random.randint(jax.random.fold_in(own, 2), (rows, 1), 0, top)
    return jnp.take_along_axis(listing, (jnp.arange(top)[None, :] + turn) % top, axis=1)


def load_shares(count, total, bound, slope, full):
    loads = [(1 << 20) // math.isqrt(standing ** slope) + 1 for standing in range(1, count + 1)]
    largest = bound if full else min(bound, max(-(-total // count), total * loads[0] // sum(loads)))
    least = 1 if total - largest >= count - 1 else 0
    holding, surplus = [largest] + [least] * (count - 1), total - largest - least * (count - 1)
    while surplus > 0:
        movable = [i for i in range(1, count) if holding[i] < largest] or [i for i in range(1, count) if holding[i] < bound]
        whole, remaining = sum([loads[i] for i in movable]), surplus
        for i in movable:
            more = min(bound - holding[i], max(1, remaining * loads[i] // whole), surplus)
            holding[i] = holding[i] + more
            surplus = surplus - more
    return np.array(holding)


def scatter_about(stream_key, dims, width, most, split=(), held_as=jnp.bfloat16):
    array = jax.random.normal(stream_key, dims, jnp.float32) * width
    if len(split) > 0:
        array = block_levels(stream_key, dims, split, -0.22, 0.18) * array
    return jnp.clip(array, min=-most, max=most).astype(held_as)


def setup_inputs(seed: int = 0) -> dict:
    key_of = jax.random.split(jax.random.key(seed), 10)
    tokens = scatter_about(key_of[0], (TOKENS, D), 1.0, 6.0, ((0, 256),))
    expert_ids_keys = jax.random.split(jax.random.fold_in(key_of[1], 1), TOKENS // TOK_DEV)
    expert_ids_turns = jax.random.permutation(jax.random.fold_in(key_of[1], 3), TOKENS // TOK_DEV)
    expert_ids = jax.vmap(lambda own, number: deal_out(jax.random.fold_in(key_of[1], 2), own, number, TOK_DEV, EXPERTS, TOP, CAP, 2))(expert_ids_keys, expert_ids_turns).reshape((TOKENS, TOP))
    gate_level = set_ends(jax.random.randint(key_of[2], (TOKENS, TOP), 0, LEVELS), jax.random.fold_in(key_of[2], 1), 0, LEVELS - 1).astype(jnp.int32)
    cost_bucket = set_ends(jax.random.randint(key_of[3], (TRAJS,), 0, BUCKETS), jax.random.fold_in(key_of[3], 1), 0, BUCKETS - 1).astype(jnp.int32)
    gate_table = jnp.clip(jnp.exp(jax.random.uniform(key_of[4], (BUCKETS, LEVELS), jnp.float32, math.log(0.05), math.log(0.6))), 0.05, 0.6)
    gate_weight = scatter_about(key_of[5], (EXPERTS, D, H), D ** -0.5, 0.125, ((0, 64), (1, 4)))
    up_weight = scatter_about(key_of[6], (EXPERTS, D, H), D ** -0.5, 0.125, ((0, 64), (1, 4)))
    down_weight = scatter_about(key_of[7], (EXPERTS, D, H), H ** -0.5, 0.21875, ((0, 64), (1, 4)))
    out_grad = scatter_about(key_of[8], (TOKENS, D), 1.0, 6.0, ((0, 256),))
    return dict(tokens=tokens, expert_ids=expert_ids, gate_level=gate_level, cost_bucket=cost_bucket, gate_table=gate_table, gate_weight=gate_weight, up_weight=up_weight, down_weight=down_weight, out_grad=out_grad)


def reference(tokens, expert_ids, gate_level, cost_bucket, gate_table, gate_weight, up_weight, down_weight, out_grad):
    assigned = TOKENS * TOP
    blocks = TOKENS // TOK_DEV
    flat_ids = expert_ids.reshape(-1).astype(jnp.int32)
    marks_hot = (flat_ids[:, None] == jnp.arange(EXPERTS, dtype=jnp.int32)[None, :]).astype(jnp.int32)
    marks_hot = marks_hot.reshape(blocks, TOK_DEV * TOP, EXPERTS)
    earlier = jnp.cumsum(marks_hot, axis=1) - marks_hot
    slot_index = jnp.sum(earlier * marks_hot, axis=2).reshape(-1).astype(jnp.int32)
    block_index = (jnp.arange(assigned, dtype=jnp.int32) // (TOK_DEV * TOP)).astype(jnp.int32)
    slot_place = ((flat_ids * blocks + block_index) * CAP + slot_index).astype(jnp.int32)
    owner_row = jnp.full((EXPERTS * blocks * CAP,), assigned, jnp.int32).at[slot_place].set(jnp.arange(assigned, dtype=jnp.int32))
    token_of = jnp.where(owner_row < assigned, owner_row // TOP, TOKENS).astype(jnp.int32).reshape(EXPERTS, blocks * CAP)
    bucket_tok = jnp.repeat(cost_bucket, TRAJ)
    gate_values = gate_table[bucket_tok[:, None], gate_level]
    gate_padded = jnp.concatenate([gate_values.reshape(-1), jnp.zeros((1,), gate_values.dtype)])
    slot_gate = gate_padded[owner_row].reshape(EXPERTS, blocks * CAP)
    zero_row = jnp.zeros((1, D), tokens.dtype)
    tokens_padded = jnp.concatenate([tokens, zero_row], axis=0)
    grad_padded = jnp.concatenate([out_grad, zero_row.astype(out_grad.dtype)], axis=0)
    contract_last = (((1,), (1,)), ((), ()))

    def grouped(values):
        return values.reshape(N_DP, (blocks * CAP) // N_DP, values.shape[-1]).astype(jnp.float32)

    def settle(partial_value):
        return lax.optimization_barrier(partial_value.astype(jnp.bfloat16)).astype(jnp.float32).sum(axis=0)

    def per_expert(totals, inputs):
        out_acc, grad_acc = totals
        rows_of, gate_of, w_gate, w_up, w_down = inputs
        expert_rows = tokens_padded[rows_of]
        gate_act = jnp.dot(expert_rows, w_gate, preferred_element_type=jnp.float32)
        up_act = jnp.dot(expert_rows, w_up, preferred_element_type=jnp.float32)
        sigmoid_gate = jax.nn.sigmoid(gate_act)
        swish_gate = gate_act * sigmoid_gate
        hidden = (swish_gate * up_act).astype(jnp.bfloat16)
        result = lax.dot_general(hidden, w_down, contract_last, preferred_element_type=jnp.float32).astype(jnp.bfloat16)
        out_acc = out_acc.at[rows_of].add(gate_of[:, None] * result.astype(jnp.float32))
        scaled = (gate_of[:, None] * grad_padded[rows_of].astype(jnp.float32)).astype(jnp.bfloat16)
        grad_hidden = jnp.dot(scaled, w_down, preferred_element_type=jnp.float32)
        grad_gate_act = (grad_hidden * up_act * sigmoid_gate * (1.0 + gate_act * (1.0 - sigmoid_gate))).astype(jnp.bfloat16)
        grad_up_act = (grad_hidden * swish_gate).astype(jnp.bfloat16)
        grad_in = (lax.dot_general(grad_gate_act, w_gate, contract_last, preferred_element_type=jnp.float32)
                   + lax.dot_general(grad_up_act, w_up, contract_last, preferred_element_type=jnp.float32)).astype(jnp.bfloat16)
        grad_acc = grad_acc.at[rows_of].add(grad_in.astype(jnp.float32))
        gate_part = jnp.einsum("gmd,gmh->gdh", grouped(expert_rows), grouped(grad_gate_act), precision=lax.Precision.HIGHEST)
        up_part = jnp.einsum("gmd,gmh->gdh", grouped(expert_rows), grouped(grad_up_act), precision=lax.Precision.HIGHEST)
        down_part = jnp.einsum("gmd,gmh->gdh", grouped(scaled), grouped(hidden), precision=lax.Precision.HIGHEST)
        return (out_acc, grad_acc), (settle(gate_part), settle(up_part), settle(down_part))

    start_totals = (jnp.zeros((TOKENS + 1, D), jnp.float32), jnp.zeros((TOKENS + 1, D), jnp.float32))
    (out_acc, grad_acc), (gate_grad, up_grad, down_grad) = lax.scan(
        per_expert, start_totals, (token_of, slot_gate, gate_weight, up_weight, down_weight))
    return (out_acc[:TOKENS].astype(jnp.bfloat16), grad_acc[:TOKENS].astype(jnp.bfloat16),
            gate_grad, up_grad, down_grad)
```

```python
import functools

import jax
import jax.numpy as jnp
from jax import lax
from jax.experimental import pallas as pl
from jax.experimental.pallas import tpu as pltpu
from jax.sharding import PartitionSpec as P


BF = jnp.bfloat16
F32 = jnp.float32
FIRST = (((0,), (0,)), ((), ()))
LAST = (((1,), (1,)), ((), ()))
VMEM = pl.BlockSpec(memory_space=pltpu.VMEM)
SMEM = pl.BlockSpec(memory_space=pltpu.SMEM)
LIMIT = 56 * 1024 * 1024


def shape_of(shape, dtype):
    return jax.ShapeDtypeStruct(shape, dtype)


def whole(kernel, outs, n_in, flops=0, nbytes=0, smem=()):
    call = pl.pallas_call(
        kernel,
        out_shape=outs,
        in_specs=[SMEM if i in smem else VMEM for i in range(n_in)],
        out_specs=[VMEM for _ in outs],
        compiler_params=pltpu.CompilerParams(vmem_limit_bytes=LIMIT),
        cost_estimate=pl.CostEstimate(flops=flops, bytes_accessed=nbytes, transcendentals=0),
    )
    return call


def placed(place, slots):
    spots = lax.broadcasted_iota(jnp.int32, (place.shape[0], slots), 1)
    return [place[:, k : k + 1] == spots for k in range(place.shape[1])]


def send_kernel(members, capacity, ids_ref, tokens_ref, rows_ref, place_ref, pick_ref):
    count, top = ids_ref.shape
    ids = ids_ref[...]
    names = lax.broadcasted_iota(jnp.int32, (count, members), 1)
    below = (
        lax.broadcasted_iota(jnp.int32, (count, count), 0)
        > lax.broadcasted_iota(jnp.int32, (count, count), 1)
    ).astype(BF)
    ahead = jnp.zeros((1, members), F32)
    pick = jnp.zeros((count, members * capacity), F32)
    spots = lax.broadcasted_iota(jnp.int32, (count, members * capacity), 1)
    for k in range(top):
        hot = (ids[:, k : k + 1] == names).astype(F32)
        earlier = jnp.dot(below, hot.astype(BF), preferred_element_type=F32) + ahead
        rank = jnp.sum(hot * earlier, axis=1, keepdims=True).astype(jnp.int32)
        ahead = ahead + jnp.sum(hot, axis=0, keepdims=True)
        place = ids[:, k : k + 1] * capacity + rank
        place_ref[:, k : k + 1] = place
        pick = pick + (place == spots).astype(F32)
    pick = pick.astype(BF)
    pick_ref[...] = pick
    rows_ref[...] = lax.dot_general(
        pick, tokens_ref[...], FIRST, preferred_element_type=F32
    ).astype(BF)


def grad_send_kernel(
    bucket_ref, place_ref, level_ref, table_ref, pick_ref, grad_ref, rows_ref, gated_ref
):
    count, _ = place_ref.shape
    slots = pick_ref.shape[1]
    levels = table_ref.shape[1]
    trajs = bucket_ref.shape[0]
    span = count // trajs
    line = lax.broadcasted_iota(jnp.int32, (count, levels), 0)
    entries = jnp.zeros((count, levels), F32)
    for j in range(trajs):
        row = table_ref[pl.ds(bucket_ref[j], 1), :]
        entries = jnp.where(line // span == j, row, entries)
    level = level_ref[...]
    at = lax.broadcasted_iota(jnp.int32, (count, levels), 1)
    gated = jnp.zeros((count, slots), F32)
    for k, hot in enumerate(placed(place_ref[...], slots)):
        gate = jnp.sum(jnp.where(level[:, k : k + 1] == at, entries, 0.0), axis=1, keepdims=True)
        gated = gated + jnp.where(hot, gate, 0.0)
    gated_ref[...] = gated
    slot_gate = jnp.sum(gated.T, axis=1, keepdims=True)
    rows = lax.dot_general(pick_ref[...], grad_ref[...], FIRST, preferred_element_type=F32)
    rows_ref[...] = (rows * slot_gate).astype(BF)


def columns(offset, size):
    return pl.ds(pl.multiple_of(offset, 128), size)


def offsets(y, n, size):
    at = lambda j: lax.rem(y + j, n) * size
    half = size // 2
    return [(at(0), size), (at(3), size), (at(1), size), (at(2), half), (at(2) + half, half)]


def forward_kernel(y_ref, rows_ref, *refs):
    gates, ups, (ga_ref, ua_ref, hid_ref) = refs[0:5], refs[5:10], refs[10:]
    gate_act = up_act = None
    for (off, size), g, u in zip(offsets(y_ref[0], 4, gates[0].shape[0]), gates, ups):
        rows = rows_ref[:, columns(off, size)]
        a = jnp.dot(rows, g[...], preferred_element_type=F32)
        b = jnp.dot(rows, u[...], preferred_element_type=F32)
        gate_act = a if gate_act is None else gate_act + a
        up_act = b if up_act is None else up_act + b
    ga_ref[...] = gate_act
    ua_ref[...] = up_act
    hid_ref[...] = (gate_act * jax.nn.sigmoid(gate_act) * up_act).astype(BF)


def backward_kernel(y_ref, rows_ref, *refs):
    downs, (ga_ref, ua_ref, gg_ref, gu_ref) = refs[0:5], refs[5:]
    grad = None
    for (off, size), d in zip(offsets(y_ref[0], 4, downs[0].shape[0]), downs):
        a = jnp.dot(rows_ref[:, columns(off, size)], d[...], preferred_element_type=F32)
        grad = a if grad is None else grad + a
    gate_act = ga_ref[...]
    s = jax.nn.sigmoid(gate_act)
    gg_ref[...] = (grad * ua_ref[...] * s * (1.0 + gate_act * (1.0 - s))).astype(BF)
    gu_ref[...] = (grad * (gate_act * s)).astype(BF)


def by_hidden(kernel, y, rows, weights, acts, outs, tile):
    depth, hidden = rows.shape[0], weights[0].shape[1]
    act = pl.BlockSpec((depth, tile), lambda h, y_ref: (0, h))
    specs = [pl.BlockSpec(rows.shape, lambda h, y_ref: (0, 0))]
    specs += [pl.BlockSpec((w.shape[0], tile), lambda h, y_ref: (0, h)) for w in weights]
    specs += [act] * len(acts)
    call = pl.pallas_call(
        kernel,
        grid_spec=pltpu.PrefetchScalarGridSpec(
            num_scalar_prefetch=1,
            grid=(hidden // tile,),
            in_specs=specs,
            out_specs=[act] * len(outs),
        ),
        out_shape=[shape_of((depth, hidden), d) for d in outs],
        compiler_params=pltpu.CompilerParams(vmem_limit_bytes=LIMIT),
        cost_estimate=pl.CostEstimate(
            flops=2 * depth * sum(w.size for w in weights),
            bytes_accessed=2 * (rows.size + sum(w.size for w in weights)) + 8 * depth * hidden,
            transcendentals=0,
        ),
    )
    return call(y, rows, *weights, *acts)


def spread_kernel(groups, y_ref, *refs):
    acts, out_ref = refs[:groups], refs[-1]
    weights = [refs[groups + 5 * i : groups + 5 * i + 5] for i in range(groups)]
    for j, (off, size) in enumerate(offsets(y_ref[0], 4, weights[0][0].shape[0])):
        total = None
        for a, w in zip(acts, weights):
            part = lax.dot_general(a[...], w[j][...], LAST, preferred_element_type=F32)
            total = part if total is None else total + part
        out_ref[:, columns(off, size)] = total.astype(BF)


def spread(y, acts, weights):
    depth = acts[0].shape[0]
    width = 4 * weights[0][0].shape[0]
    flat = [w for ws in weights for w in ws]
    return whole(
        functools.partial(spread_kernel, len(acts)),
        [shape_of((depth, width), BF)],
        1 + len(acts) + len(flat),
        flops=2 * depth * sum(w.size for w in flat),
        nbytes=2 * (depth * width + sum(w.size for w in flat)),
        smem=(0,),
    )(y, *acts, *flat)[0]


def partial_kernel(parts, y_ref, rows_ref, *refs):
    acts, (own_ref, up_a, up_b, dn_a, dn_b, far_a, far_b) = refs[:parts], refs[parts:]
    size = own_ref.shape[0]
    half = size // 2
    y = y_ref[0]
    spots = [(0, 0, own_ref, size), (1, 0, up_a, half), (1, half, up_b, half)]
    spots += [(3, 0, dn_a, half), (3, half, dn_b, half), (2, 0, far_a, half), (2, half, far_b, half)]
    for j, lead, ref, length in spots:
        rows = rows_ref[:, columns(lax.rem(y + j, 4) * size + lead, length)]
        at = 0
        for a in acts:
            ref[:, at : at + a.shape[1]] = lax.dot_general(
                rows, a[...], FIRST, preferred_element_type=F32
            ).astype(BF)
            at += a.shape[1]


def partials(y, rows, acts, size):
    wide = sum(a.shape[1] for a in acts)
    half = shape_of((size // 2, wide), BF)
    return whole(
        functools.partial(partial_kernel, len(acts)),
        [shape_of((size, wide), BF)] + [half] * 6,
        2 + len(acts),
        flops=2 * rows.size * wide,
        nbytes=2 * (rows.size + 4 * size * wide),
        smem=(0,),
    )(y, rows, *acts)


def output_kernel(gated_ref, rows_ref, out_ref):
    gated = gated_ref[...]
    rows = rows_ref[...]
    total = None
    for _ in range(3):
        piece = gated.astype(BF)
        gated = gated - piece.astype(F32)
        part = jnp.dot(piece, rows, preferred_element_type=F32)
        total = part if total is None else total + part
    out_ref[...] = total.astype(BF)


def token_grad_kernel(pick_ref, rows_ref, out_ref):
    out_ref[...] = jnp.dot(pick_ref[...], rows_ref[...], preferred_element_type=F32).astype(BF)


def move_rows(rows, members):
    depth, width = rows.shape
    buffer = rows.reshape(members, depth // members, width)
    moved = lax.all_to_all(buffer, "expert", split_axis=0, concat_axis=0, tiled=True)
    return moved.reshape(depth, width)


def shift(x, by):
    return lax.ppermute(x, "dp", [(i, (i + by) % 4) for i in range(4)])


def ring_gather(shard):
    half = shard.shape[0] // 2
    below, above = shift(shard, 1), shift(shard, -1)
    far_a = shift(below[:half], 1)
    far_b = shift(above[half:], -1)
    return [shard, below, above, far_a, far_b]


def ring_sum(own, up_a, up_b, dn_a, dn_b, far_a, far_b):
    got_a, got_b = shift(far_a, 1), shift(far_b, -1)
    below_b, above_a = shift(up_b, 1), shift(dn_a, -1)
    up_a = (up_a.astype(F32) + got_a.astype(F32)).astype(BF)
    dn_b = (dn_b.astype(F32) + got_b.astype(F32)).astype(BF)
    below_a, above_b = shift(up_a, 1), shift(dn_b, -1)
    half = own.shape[0] // 2
    low = own[:half].astype(F32) + below_a.astype(F32) + above_a.astype(F32)
    high = own[half:].astype(F32) + below_b.astype(F32) + above_b.astype(F32)
    return jnp.concatenate([low, high], axis=0)


def shards(
    tokens,
    expert_ids,
    gate_level,
    cost_bucket,
    gate_table,
    gate_weight,
    up_weight,
    down_weight,
    out_grad,
):
    count, width = tokens.shape
    top = expert_ids.shape[1]
    members = lax.axis_size("expert")
    capacity = min(count, 4 * count * top // (3 * members))
    slots = members * capacity
    size, hidden = gate_weight.shape[1:]
    y = lax.axis_index("dp").astype(jnp.int32).reshape(1)

    rows, place, pick = whole(
        functools.partial(send_kernel, members, capacity),
        [
            shape_of((slots, width), BF),
            shape_of((count, top), jnp.int32),
            shape_of((count, slots), BF),
        ],
        2,
        nbytes=3 * 2**20,
    )(expert_ids, tokens)
    expert_rows = move_rows(rows, members)
    g_rows, gated = whole(
        grad_send_kernel,
        [shape_of((slots, width), BF), shape_of((count, slots), F32)],
        6,
        nbytes=3 * 2**20,
        smem=(0,),
    )(cost_bucket, place, gate_level, gate_table, pick, out_grad)
    grad_rows = move_rows(g_rows, members)

    w_gate, w_up, w_down = [ring_gather(w[0]) for w in (gate_weight, up_weight, down_weight)]

    gate_act, up_act, hid = by_hidden(
        forward_kernel, y, expert_rows, w_gate + w_up, [], [F32, F32, BF], 256
    )
    result = spread(y, [hid], [w_down])
    returned = move_rows(result, members)

    grad_gate, grad_up = by_hidden(
        backward_kernel, y, grad_rows, w_down, [gate_act, up_act], [BF, BF], 256
    )
    grad_in = spread(y, [grad_gate, grad_up], [w_gate, w_up])
    grad_in, returned = lax.optimization_barrier((grad_in, returned))
    grad_back = move_rows(grad_in, members)
    output = whole(output_kernel, [shape_of((count, width), BF)], 2, nbytes=3 * 2**20)(
        gated, returned
    )[0]
    token_grad = whole(
        token_grad_kernel, [shape_of((count, width), BF)], 2, nbytes=3 * 2**20
    )(pick, grad_back)[0]

    down_grad = ring_sum(*partials(y, grad_rows, [hid], size))
    both = ring_sum(*partials(y, expert_rows, [grad_gate, grad_up], size))
    return (output, token_grad, both[None, :, :hidden], both[None, :, hidden:], down_grad[None])


def solution(mesh):
    both = ("dp", "expert")
    return jax.shard_map(
        shards,
        mesh=mesh,
        in_specs=(
            P(both, None),
            P(both, None),
            P(both, None),
            P(both),
            P(),
            P("expert", "dp", None),
            P("expert", "dp", None),
            P("expert", "dp", None),
            P(both, None),
        ),
        out_specs=(
            P(both, None),
            P(both, None),
            P("expert", "dp", None),
            P("expert", "dp", None),
            P("expert", "dp", None),
        ),
        check_vma=False,
    )
```

```python
import functools

import jax
import jax.numpy as jnp
from jax import lax
from jax.experimental import pallas as pl
from jax.experimental.pallas import tpu as pltpu
from jax.sharding import PartitionSpec as P


BF = jnp.bfloat16
F32 = jnp.float32
FIRST = (((0,), (0,)), ((), ()))
LAST = (((1,), (1,)), ((), ()))
VMEM = pl.BlockSpec(memory_space=pltpu.VMEM)
SMEM = pl.BlockSpec(memory_space=pltpu.SMEM)
LIMIT = 67_043_328


def shape_of(shape, dtype):
    return jax.ShapeDtypeStruct(shape, dtype)


def whole(kernel, outs, n_in, flops=0, nbytes=0, smem=()):
    call = pl.pallas_call(
        kernel,
        out_shape=outs,
        in_specs=[SMEM if i in smem else VMEM for i in range(n_in)],
        out_specs=[VMEM for _ in outs],
        compiler_params=pltpu.CompilerParams(vmem_limit_bytes=LIMIT),
        cost_estimate=pl.CostEstimate(flops=flops, bytes_accessed=nbytes, transcendentals=0),
    )
    return call


def chosen(place, slots):
    spots = lax.broadcasted_iota(jnp.int32, (slots, place.shape[1]), 0)
    return [place[k : k + 1, :] == spots for k in range(place.shape[0])]


def added(terms):
    total = terms[0]
    for term in terms[1:]:
        total = total + term
    return total


def send_kernel(members, capacity, ids_ref, tokens_ref, rows_ref, place_ref):
    top, count = ids_ref.shape
    names = lax.broadcasted_iota(jnp.int32, (members, count), 0)
    before = (
        lax.broadcasted_iota(jnp.int32, (count, count), 0)
        < lax.broadcasted_iota(jnp.int32, (count, count), 1)
    ).astype(BF)
    ahead = jnp.zeros((members, 1), F32)
    places = []
    for k in range(top):
        ids = ids_ref[k : k + 1, :]
        hot = (ids == names).astype(F32)
        earlier = jnp.dot(hot.astype(BF), before, preferred_element_type=F32) + ahead
        rank = jnp.sum(hot * earlier, axis=0, keepdims=True).astype(jnp.int32)
        ahead = ahead + jnp.sum(hot, axis=1, keepdims=True)
        places.append(ids * capacity + rank)
        place_ref[k : k + 1, :] = places[-1]
    spots = lax.broadcasted_iota(jnp.int32, (members * capacity, count), 0)
    pick = added([(place == spots).astype(F32) for place in places]).astype(BF)
    rows_ref[...] = jnp.dot(pick, tokens_ref[...], preferred_element_type=F32).astype(BF)


def grad_send_kernel(bucket_ref, table_ref, place_ref, level_ref, grad_ref, rows_ref, gate_ref):
    top, count = place_ref.shape
    slots = rows_ref.shape[0]
    trajs = bucket_ref.shape[0]
    level = level_ref[...]
    traj = lax.broadcasted_iota(jnp.int32, (top, count), 1) // (count // trajs)
    gate = jnp.zeros((top, count), F32)
    for at in range(table_ref.shape[1]):
        entry = jnp.zeros((top, count), F32)
        for j in range(trajs):
            entry = jnp.where(traj == j, table_ref[bucket_ref[j], at], entry)
        gate = jnp.where(level == at, entry, gate)
    gate_ref[...] = gate
    hots = chosen(place_ref[...], slots)
    pick = added([hot.astype(F32) for hot in hots]).astype(BF)
    gated = added([jnp.where(hot, gate[k : k + 1, :], 0.0) for k, hot in enumerate(hots)])
    slot_gate = jnp.sum(gated, axis=1, keepdims=True)
    rows = jnp.dot(pick, grad_ref[...], preferred_element_type=F32)
    rows_ref[...] = (rows * slot_gate).astype(BF)


def pick_kernel(place_ref, gate_ref, pick_ref, gated_ref):
    hots = chosen(place_ref[...], pick_ref.shape[1])
    pick_ref[...] = added([hot.astype(F32) for hot in hots]).T.astype(BF)
    gate = gate_ref[...]
    gated_ref[...] = added(
        [jnp.where(hot, gate[k : k + 1, :], 0.0) for k, hot in enumerate(hots)]
    ).T


def split_kernel(gated_ref, pieces_ref):
    rest = gated_ref[...]
    for i in range(pieces_ref.shape[0]):
        piece = rest.astype(BF)
        pieces_ref[i] = piece
        rest = rest - piece.astype(F32)


def columns(offset, size):
    return pl.ds(pl.multiple_of(offset, 128), size)


def offsets(y, n, size):
    at = lambda j: lax.rem(y + j, n) * size
    half = size // 2
    return [(at(0), size), (at(3), size), (at(1), size), (at(2), half), (at(2) + half, half)]


def forward_kernel(y_ref, rows_ref, *refs):
    gates, ups, (ga_ref, ua_ref, hid_ref) = refs[0:5], refs[5:10], refs[10:]
    gate_act = up_act = None
    for (off, size), g, u in zip(offsets(y_ref[0], 4, gates[0].shape[0]), gates, ups):
        rows = rows_ref[:, columns(off, size)]
        a = jnp.dot(rows, g[...], preferred_element_type=F32)
        b = jnp.dot(rows, u[...], preferred_element_type=F32)
        gate_act = a if gate_act is None else gate_act + a
        up_act = b if up_act is None else up_act + b
    ga_ref[...] = gate_act
    ua_ref[...] = up_act
    hid_ref[...] = (gate_act * jax.nn.sigmoid(gate_act) * up_act).astype(BF)


def backward_kernel(y_ref, rows_ref, *refs):
    downs, (ga_ref, ua_ref, gg_ref, gu_ref) = refs[0:5], refs[5:]
    grad = None
    for (off, size), d in zip(offsets(y_ref[0], 4, downs[0].shape[0]), downs):
        a = jnp.dot(rows_ref[:, columns(off, size)], d[...], preferred_element_type=F32)
        grad = a if grad is None else grad + a
    gate_act = ga_ref[...]
    s = jax.nn.sigmoid(gate_act)
    gg_ref[...] = (grad * ua_ref[...] * s * (1.0 + gate_act * (1.0 - s))).astype(BF)
    gu_ref[...] = (grad * (gate_act * s)).astype(BF)


def by_hidden(kernel, y, rows, weights, acts, outs, tile):
    depth, hidden = rows.shape[0], weights[0][0].shape[2]
    act = pl.BlockSpec((depth, tile), lambda h, y_ref: (0, h))
    specs = [pl.BlockSpec(rows.shape, lambda h, y_ref: (0, 0))]
    for w, i in weights:
        specs.append(
            pl.BlockSpec((None, w.shape[1], tile), lambda h, y_ref, i=i: (i, 0, h))
        )
    specs += [act] * len(acts)
    size = sum(w.shape[1] * w.shape[2] for w, _ in weights)
    call = pl.pallas_call(
        kernel,
        grid_spec=pltpu.PrefetchScalarGridSpec(
            num_scalar_prefetch=1,
            grid=(hidden // tile,),
            in_specs=specs,
            out_specs=[act] * len(outs),
        ),
        out_shape=[shape_of((depth, hidden), d) for d in outs],
        compiler_params=pltpu.CompilerParams(vmem_limit_bytes=LIMIT),
        cost_estimate=pl.CostEstimate(
            flops=2 * depth * size,
            bytes_accessed=2 * (rows.size + size) + 8 * depth * hidden,
            transcendentals=0,
        ),
    )
    return call(y, rows, *[w for w, _ in weights], *acts)


def spread_kernel(groups, y_ref, *refs):
    acts, out_ref = refs[:groups], refs[-1]
    weights = [refs[groups + 5 * i : groups + 5 * i + 5] for i in range(groups)]
    for j, (off, size) in enumerate(offsets(y_ref[0], 4, weights[0][0].shape[0])):
        total = None
        for a, w in zip(acts, weights):
            part = lax.dot_general(a[...], w[j][...], LAST, preferred_element_type=F32)
            total = part if total is None else total + part
        out_ref[:, columns(off, size)] = total.astype(BF)


def spread(y, acts, weights):
    depth, hidden = acts[0].shape
    width = 4 * weights[0][0][0].shape[1]
    flat = [w for ws in weights for w in ws]
    act = pl.BlockSpec((depth, hidden), lambda g, y_ref: (0, 0))
    call = pl.pallas_call(
        functools.partial(spread_kernel, len(acts)),
        grid_spec=pltpu.PrefetchScalarGridSpec(
            num_scalar_prefetch=1,
            grid=(1,),
            in_specs=[act] * len(acts)
            + [
                pl.BlockSpec((None, w.shape[1], hidden), lambda g, y_ref, i=i: (i, 0, 0))
                for w, i in flat
            ],
            out_specs=pl.BlockSpec((depth, width), lambda g, y_ref: (0, 0)),
        ),
        out_shape=shape_of((depth, width), BF),
        compiler_params=pltpu.CompilerParams(vmem_limit_bytes=LIMIT),
        cost_estimate=pl.CostEstimate(
            flops=2 * depth * width * hidden * len(acts),
            bytes_accessed=2 * width * (depth + hidden * len(acts)),
            transcendentals=0,
        ),
    )
    return call(y, *acts, *[w for w, _ in flat])


def partial_kernel(parts, y_ref, rows_ref, *refs):
    acts, (own_ref, up_ref, dn_ref, up_a, dn_b) = refs[:parts], refs[parts:]
    size = own_ref.shape[0]
    half = size // 2
    y = y_ref[0]
    spots = [(2, 0, up_ref, 0, half), (1, half, up_ref, half, half)]
    spots += [(2, half, dn_ref, 0, half), (3, 0, dn_ref, half, half)]
    spots += [(1, 0, up_a, 0, half), (3, half, dn_b, 0, half), (0, 0, own_ref, 0, size)]
    for j, lead, ref, top, length in spots:
        rows = rows_ref[:, columns(lax.rem(y + j, 4) * size + lead, length)]
        at = 0
        for a in acts:
            ref[top : top + length, at : at + a.shape[1]] = lax.dot_general(
                rows, a[...], FIRST, preferred_element_type=F32
            ).astype(BF)
            at += a.shape[1]


def partials(y, rows, acts, size):
    wide = sum(a.shape[1] for a in acts)
    full, half = shape_of((size, wide), BF), shape_of((size // 2, wide), BF)
    return whole(
        functools.partial(partial_kernel, len(acts)),
        [full, full, full, half, half],
        2 + len(acts),
        flops=2 * rows.size * wide,
        nbytes=2 * (rows.size + 4 * size * wide),
        smem=(0,),
    )(y, rows, *acts)


def sum_kernel(own_ref, up_ref, dn_ref, below_ref, above_ref, *outs):
    half = below_ref.shape[0]
    hidden = outs[0].shape[2]
    for i, out in enumerate(outs):
        at = slice(i * hidden, (i + 1) * hidden)
        out[0, :half] = (
            own_ref[:half, at].astype(F32)
            + below_ref[:, at].astype(F32)
            + dn_ref[half:, at].astype(F32)
        )
        out[0, half:] = (
            own_ref[half:, at].astype(F32)
            + up_ref[half:, at].astype(F32)
            + above_ref[:, at].astype(F32)
        )


def output_kernel(pieces_ref, rows_ref, out_ref):
    rows = rows_ref[...]
    out_ref[...] = added(
        [
            jnp.dot(pieces_ref[i], rows, preferred_element_type=F32)
            for i in range(pieces_ref.shape[0])
        ]
    ).astype(BF)


def token_grad_kernel(pick_ref, rows_ref, out_ref):
    out_ref[...] = jnp.dot(pick_ref[...], rows_ref[...], preferred_element_type=F32).astype(BF)


def move_rows(rows, members):
    depth, width = rows.shape
    buffer = rows.reshape(members, depth // members, width)
    moved = lax.all_to_all(buffer, "expert", split_axis=0, concat_axis=0, tiled=True)
    return moved.reshape(depth, width)


def shift(x, by):
    return lax.ppermute(x, "dp", [(i, (i + by) % 4) for i in range(4)])


def ring_gather(weights):
    shard = jnp.concatenate(weights, axis=0)
    half = shard.shape[1] // 2
    below, above = shift(shard, 1), shift(shard, -1)
    far_a = shift(below[:, :half], 1)
    far_b = shift(above[:, half:], -1)
    return [
        [(w, 0), (below, i), (above, i), (far_a, i), (far_b, i)] for i, w in enumerate(weights)
    ]


def ring_sum(parts, own, up, dn, up_a, dn_b):
    size, wide = own.shape
    half = size // 2
    got_up, got_dn = shift(up, 1), shift(dn, -1)
    up_a = (up_a.astype(F32) + got_up[:half].astype(F32)).astype(BF)
    dn_b = (dn_b.astype(F32) + got_dn[:half].astype(F32)).astype(BF)
    below, above = shift(up_a, 1), shift(dn_b, -1)
    return whole(
        sum_kernel, [shape_of((1, size, wide // parts), F32)] * parts, 5, nbytes=12 * size * wide
    )(own, got_up, got_dn, below, above)


def shards(
    tokens,
    expert_ids,
    gate_level,
    cost_bucket,
    gate_table,
    gate_weight,
    up_weight,
    down_weight,
    out_grad,
):
    count, width = tokens.shape
    top = expert_ids.shape[1]
    members = lax.axis_size("expert")
    capacity = min(count, 4 * count * top // (3 * members))
    slots = members * capacity
    size, _ = gate_weight.shape[1:]
    y = lax.axis_index("dp").astype(jnp.int32).reshape(1)

    rows, place = whole(
        functools.partial(send_kernel, members, capacity),
        [shape_of((slots, width), BF), shape_of((top, count), jnp.int32)],
        2,
        nbytes=3 * 2**20,
    )(expert_ids.T, tokens)
    expert_rows = move_rows(rows, members)
    g_rows, gates = whole(
        grad_send_kernel,
        [shape_of((slots, width), BF), shape_of((top, count), F32)],
        5,
        nbytes=3 * 2**20,
        smem=(0, 1),
    )(cost_bucket, gate_table, place, gate_level.T, out_grad)
    grad_rows = move_rows(g_rows, members)
    pick, gated = whole(
        pick_kernel, [shape_of((count, slots), BF), shape_of((count, slots), F32)], 2, nbytes=2**20
    )(place, gates)
    pieces = whole(split_kernel, [shape_of((3, count, slots), BF)], 1, nbytes=2**20)(gated)[0]

    w_gate, w_up, w_down = ring_gather([gate_weight, up_weight, down_weight])
    gate_act, up_act, hid = by_hidden(
        forward_kernel, y, expert_rows, w_gate + w_up, [], [F32, F32, BF], 256
    )
    result = spread(y, [hid], [w_down])
    returned = move_rows(result, members)

    grad_gate, grad_up = by_hidden(
        backward_kernel, y, grad_rows, w_down, [gate_act, up_act], [BF, BF], 256
    )
    grad_in = spread(y, [grad_gate, grad_up], [w_gate, w_up])
    grad_back = move_rows(grad_in, members)
    output = whole(output_kernel, [shape_of((count, width), BF)], 2, nbytes=3 * 2**20)(
        pieces, returned
    )[0]
    token_grad = whole(
        token_grad_kernel, [shape_of((count, width), BF)], 2, nbytes=3 * 2**20
    )(pick, grad_back)[0]

    down_grad = ring_sum(1, *partials(y, grad_rows, [hid], size))[0]
    gate_grad, up_grad = ring_sum(2, *partials(y, expert_rows, [grad_gate, grad_up], size))
    return (output, token_grad, gate_grad, up_grad, down_grad)


def solution(mesh):
    both = ("dp", "expert")
    return jax.shard_map(
        shards,
        mesh=mesh,
        in_specs=(
            P(both, None),
            P(both, None),
            P(both, None),
            P(both),
            P(),
            P("expert", "dp", None),
            P("expert", "dp", None),
            P("expert", "dp", None),
            P(both, None),
        ),
        out_specs=(
            P(both, None),
            P(both, None),
            P("expert", "dp", None),
            P("expert", "dp", None),
            P("expert", "dp", None),
        ),
        check_vma=False,
    )
```

```python
import functools

import jax
import jax.numpy as jnp
from jax import lax
from jax.experimental import pallas as pl
from jax.experimental.pallas import tpu as pltpu
from jax.sharding import PartitionSpec as P


BF = jnp.bfloat16
F32 = jnp.float32
FIRST = (((0,), (0,)), ((), ()))
LAST = (((1,), (1,)), ((), ()))
VMEM = pl.BlockSpec(memory_space=pltpu.VMEM)
SMEM = pl.BlockSpec(memory_space=pltpu.SMEM)
LIMIT = 67_043_328


def shape_of(shape, dtype):
    return jax.ShapeDtypeStruct(shape, dtype)


def whole(kernel, outs, n_in, flops=0, nbytes=0, smem=(), limit=LIMIT):
    call = pl.pallas_call(
        kernel,
        out_shape=outs,
        in_specs=[SMEM if i in smem else VMEM for i in range(n_in)],
        out_specs=[VMEM for _ in outs],
        compiler_params=pltpu.CompilerParams(vmem_limit_bytes=limit),
        cost_estimate=pl.CostEstimate(flops=flops, bytes_accessed=nbytes, transcendentals=0),
    )
    return call


def chosen(place, slots):
    spots = lax.broadcasted_iota(jnp.int32, (slots, place.shape[1]), 0)
    return [place[k : k + 1, :] == spots for k in range(place.shape[0])]


def added(terms):
    total = terms[0]
    for term in terms[1:]:
        total = total + term
    return total


def send_kernel(members, capacity, ids_ref, tokens_ref, rows_ref, place_ref):
    top, count = ids_ref.shape
    names = lax.broadcasted_iota(jnp.int32, (members, count), 0)
    before = (
        lax.broadcasted_iota(jnp.int32, (count, count), 0)
        < lax.broadcasted_iota(jnp.int32, (count, count), 1)
    ).astype(BF)
    ahead = jnp.zeros((members, 1), F32)
    places = []
    for k in range(top):
        ids = ids_ref[k : k + 1, :]
        hot = (ids == names).astype(F32)
        earlier = jnp.dot(hot.astype(BF), before, preferred_element_type=F32) + ahead
        rank = jnp.sum(hot * earlier, axis=0, keepdims=True).astype(jnp.int32)
        ahead = ahead + jnp.sum(hot, axis=1, keepdims=True)
        places.append(ids * capacity + rank)
        place_ref[k : k + 1, :] = places[-1]
    spots = lax.broadcasted_iota(jnp.int32, (members * capacity, count), 0)
    pick = added([(place == spots).astype(F32) for place in places]).astype(BF)
    rows_ref[...] = jnp.dot(pick, tokens_ref[...], preferred_element_type=F32).astype(BF)


def grad_send_kernel(bucket_ref, table_ref, place_ref, level_ref, grad_ref, rows_ref, gate_ref):
    top, count = place_ref.shape
    slots = rows_ref.shape[0]
    trajs = bucket_ref.shape[0]
    level = level_ref[...]
    traj = lax.broadcasted_iota(jnp.int32, (top, count), 1) // (count // trajs)
    gate = jnp.zeros((top, count), F32)
    for at in range(table_ref.shape[1]):
        entry = jnp.zeros((top, count), F32)
        for j in range(trajs):
            entry = jnp.where(traj == j, table_ref[bucket_ref[j], at], entry)
        gate = jnp.where(level == at, entry, gate)
    gate_ref[...] = gate
    hots = chosen(place_ref[...], slots)
    pick = added([hot.astype(F32) for hot in hots]).astype(BF)
    gated = added([jnp.where(hot, gate[k : k + 1, :], 0.0) for k, hot in enumerate(hots)])
    slot_gate = jnp.sum(gated, axis=1, keepdims=True)
    rows = jnp.dot(pick, grad_ref[...], preferred_element_type=F32)
    rows_ref[...] = (rows * slot_gate).astype(BF)


def pick_kernel(place_ref, gate_ref, pick_ref, gated_ref):
    hots = chosen(place_ref[...], pick_ref.shape[1])
    pick_ref[...] = added([hot.astype(F32) for hot in hots]).T.astype(BF)
    gate = gate_ref[...]
    gated_ref[...] = added(
        [jnp.where(hot, gate[k : k + 1, :], 0.0) for k, hot in enumerate(hots)]
    ).T


def split_kernel(gated_ref, pieces_ref):
    rest = gated_ref[...]
    for i in range(pieces_ref.shape[0]):
        piece = rest.astype(BF)
        pieces_ref[i] = piece
        rest = rest - piece.astype(F32)


def columns(offset, size):
    return pl.ds(pl.multiple_of(offset, 128), size)


def offsets(y, n, size):
    at = lambda j: lax.rem(y + j, n) * size
    half = size // 2
    return [(at(0), size), (at(3), size), (at(1), size), (at(2), half), (at(2) + half, half)]


def forward_kernel(y_ref, rows_ref, *refs):
    gates, ups, (ga_ref, ua_ref, hid_ref) = refs[0:5], refs[5:10], refs[10:]
    gate_act = up_act = None
    for (off, size), g, u in zip(offsets(y_ref[0], 4, gates[0].shape[0]), gates, ups):
        rows = rows_ref[:, columns(off, size)]
        a = jnp.dot(rows, g[...], preferred_element_type=F32)
        b = jnp.dot(rows, u[...], preferred_element_type=F32)
        gate_act = a if gate_act is None else gate_act + a
        up_act = b if up_act is None else up_act + b
    ga_ref[...] = gate_act
    ua_ref[...] = up_act
    hid_ref[...] = (gate_act * jax.nn.sigmoid(gate_act) * up_act).astype(BF)


def backward_kernel(y_ref, rows_ref, *refs):
    downs, (ga_ref, ua_ref, gg_ref, gu_ref) = refs[0:5], refs[5:]
    grad = None
    for (off, size), d in zip(offsets(y_ref[0], 4, downs[0].shape[0]), downs):
        a = jnp.dot(rows_ref[:, columns(off, size)], d[...], preferred_element_type=F32)
        grad = a if grad is None else grad + a
    gate_act = ga_ref[...]
    s = jax.nn.sigmoid(gate_act)
    gg_ref[...] = (grad * ua_ref[...] * s * (1.0 + gate_act * (1.0 - s))).astype(BF)
    gu_ref[...] = (grad * (gate_act * s)).astype(BF)


def by_hidden(kernel, y, rows, weights, acts, outs, tile):
    depth, hidden = rows.shape[0], weights[0][0].shape[2]
    act = pl.BlockSpec((depth, tile), lambda h, y_ref: (0, h))
    specs = [pl.BlockSpec(rows.shape, lambda h, y_ref: (0, 0))]
    for w, i in weights:
        specs.append(
            pl.BlockSpec((None, w.shape[1], tile), lambda h, y_ref, i=i: (i, 0, h))
        )
    specs += [act] * len(acts)
    size = sum(w.shape[1] * w.shape[2] for w, _ in weights)
    call = pl.pallas_call(
        kernel,
        grid_spec=pltpu.PrefetchScalarGridSpec(
            num_scalar_prefetch=1,
            grid=(hidden // tile,),
            in_specs=specs,
            out_specs=[act] * len(outs),
        ),
        out_shape=[shape_of((depth, hidden), d) for d in outs],
        compiler_params=pltpu.CompilerParams(vmem_limit_bytes=LIMIT),
        cost_estimate=pl.CostEstimate(
            flops=2 * depth * size,
            bytes_accessed=2 * (rows.size + size) + 8 * depth * hidden,
            transcendentals=0,
        ),
    )
    return call(y, rows, *[w for w, _ in weights], *acts)


def spread_kernel(groups, y_ref, *refs):
    acts, out_ref = refs[:groups], refs[-1]
    weights = [refs[groups + 5 * i : groups + 5 * i + 5] for i in range(groups)]
    for j, (off, size) in enumerate(offsets(y_ref[0], 4, weights[0][0].shape[0])):
        total = None
        for a, w in zip(acts, weights):
            part = lax.dot_general(a[...], w[j][...], LAST, preferred_element_type=F32)
            total = part if total is None else total + part
        out_ref[:, columns(off, size)] = total.astype(BF)


def spread(y, acts, weights):
    depth, hidden = acts[0].shape
    width = 4 * weights[0][0][0].shape[1]
    flat = [w for ws in weights for w in ws]
    act = pl.BlockSpec((depth, hidden), lambda g, y_ref: (0, 0))
    call = pl.pallas_call(
        functools.partial(spread_kernel, len(acts)),
        grid_spec=pltpu.PrefetchScalarGridSpec(
            num_scalar_prefetch=1,
            grid=(1,),
            in_specs=[act] * len(acts)
            + [
                pl.BlockSpec((None, w.shape[1], hidden), lambda g, y_ref, i=i: (i, 0, 0))
                for w, i in flat
            ],
            out_specs=pl.BlockSpec((depth, width), lambda g, y_ref: (0, 0)),
        ),
        out_shape=shape_of((depth, width), BF),
        compiler_params=pltpu.CompilerParams(vmem_limit_bytes=LIMIT),
        cost_estimate=pl.CostEstimate(
            flops=2 * depth * width * hidden * len(acts),
            bytes_accessed=2 * width * (depth + hidden * len(acts)),
            transcendentals=0,
        ),
    )
    return call(y, *acts, *[w for w, _ in flat])


def partial_kernel(parts, y_ref, rows_ref, *refs):
    acts, (own_ref, up_ref, dn_ref, up_a, dn_b) = refs[:parts], refs[parts:]
    size = own_ref.shape[0]
    half = size // 2
    y = y_ref[0]
    spots = [(2, 0, up_ref, 0, half), (1, half, up_ref, half, half)]
    spots += [(2, half, dn_ref, 0, half), (3, 0, dn_ref, half, half)]
    spots += [(1, 0, up_a, 0, half), (3, half, dn_b, 0, half), (0, 0, own_ref, 0, size)]
    for j, lead, ref, top, length in spots:
        rows = rows_ref[:, columns(lax.rem(y + j, 4) * size + lead, length)]
        at = 0
        for a in acts:
            ref[top : top + length, at : at + a.shape[1]] = lax.dot_general(
                rows, a[...], FIRST, preferred_element_type=F32
            ).astype(BF)
            at += a.shape[1]


def partials(y, rows, acts, size):
    wide = sum(a.shape[1] for a in acts)
    full, half = shape_of((size, wide), BF), shape_of((size // 2, wide), BF)
    return whole(
        functools.partial(partial_kernel, len(acts)),
        [full, full, full, half, half],
        2 + len(acts),
        flops=2 * rows.size * wide,
        nbytes=2 * (rows.size + 4 * size * wide),
        smem=(0,),
    )(y, rows, *acts)


def sum_kernel(own_ref, up_ref, dn_ref, below_ref, above_ref, *outs):
    half = below_ref.shape[0]
    hidden = outs[0].shape[2]
    for i, out in enumerate(outs):
        at = slice(i * hidden, (i + 1) * hidden)
        out[0, :half] = (
            own_ref[:half, at].astype(F32)
            + below_ref[:, at].astype(F32)
            + dn_ref[half:, at].astype(F32)
        )
        out[0, half:] = (
            own_ref[half:, at].astype(F32)
            + up_ref[half:, at].astype(F32)
            + above_ref[:, at].astype(F32)
        )


def output_kernel(pieces_ref, rows_ref, out_ref):
    rows = rows_ref[...]
    out_ref[...] = added(
        [
            jnp.dot(pieces_ref[i], rows, preferred_element_type=F32)
            for i in range(pieces_ref.shape[0])
        ]
    ).astype(BF)


def token_grad_kernel(pick_ref, rows_ref, out_ref):
    out_ref[...] = jnp.dot(pick_ref[...], rows_ref[...], preferred_element_type=F32).astype(BF)


def move_rows(rows, members):
    depth, width = rows.shape
    buffer = rows.reshape(members, depth // members, width)
    moved = lax.all_to_all(buffer, "expert", split_axis=0, concat_axis=0, tiled=True)
    return moved.reshape(depth, width)


def shift(x, by):
    return lax.ppermute(x, "dp", [(i, (i + by) % 4) for i in range(4)])


def ring_gather(weights):
    shard = jnp.concatenate(weights, axis=0)
    half = shard.shape[1] // 2
    below, above = shift(shard, 1), shift(shard, -1)
    far_a = shift(below[:, :half], 1)
    far_b = shift(above[:, half:], -1)
    return [
        [(w, 0), (below, i), (above, i), (far_a, i), (far_b, i)] for i, w in enumerate(weights)
    ]


def ring_sum(parts, own, up, dn, up_a, dn_b):
    size, wide = own.shape
    half = size // 2
    got_up, got_dn = shift(up, 1), shift(dn, -1)
    up_a = (up_a.astype(F32) + got_up[:half].astype(F32)).astype(BF)
    dn_b = (dn_b.astype(F32) + got_dn[:half].astype(F32)).astype(BF)
    below, above = shift(up_a, 1), shift(dn_b, -1)
    return whole(
        sum_kernel,
        [shape_of((1, size, wide // parts), F32)] * parts,
        5,
        nbytes=12 * size * wide,
        limit=24 * 2**20,
    )(own, got_up, got_dn, below, above)


def shards(
    tokens,
    expert_ids,
    gate_level,
    cost_bucket,
    gate_table,
    gate_weight,
    up_weight,
    down_weight,
    out_grad,
):
    count, width = tokens.shape
    top = expert_ids.shape[1]
    members = lax.axis_size("expert")
    capacity = min(count, 4 * count * top // (3 * members))
    slots = members * capacity
    size, _ = gate_weight.shape[1:]
    y = lax.axis_index("dp").astype(jnp.int32).reshape(1)

    rows, place = whole(
        functools.partial(send_kernel, members, capacity),
        [shape_of((slots, width), BF), shape_of((top, count), jnp.int32)],
        2,
        nbytes=3 * 2**20,
    )(expert_ids.T, tokens)
    expert_rows = move_rows(rows, members)
    g_rows, gates = whole(
        grad_send_kernel,
        [shape_of((slots, width), BF), shape_of((top, count), F32)],
        5,
        nbytes=3 * 2**20,
        smem=(0, 1),
    )(cost_bucket, gate_table, place, gate_level.T, out_grad)
    grad_rows = move_rows(g_rows, members)
    pick, gated = whole(
        pick_kernel, [shape_of((count, slots), BF), shape_of((count, slots), F32)], 2, nbytes=2**20
    )(place, gates)
    pieces = whole(split_kernel, [shape_of((3, count, slots), BF)], 1, nbytes=2**20)(gated)[0]

    w_gate, w_up, w_down = ring_gather([gate_weight, up_weight, down_weight])
    gate_act, up_act, hid = by_hidden(
        forward_kernel, y, expert_rows, w_gate + w_up, [], [F32, F32, BF], 256
    )
    result = spread(y, [hid], [w_down])
    returned = move_rows(result, members)

    grad_gate, grad_up = by_hidden(
        backward_kernel, y, grad_rows, w_down, [gate_act, up_act], [BF, BF], 256
    )
    grad_in = spread(y, [grad_gate, grad_up], [w_gate, w_up])
    grad_back = move_rows(grad_in, members)
    output = whole(output_kernel, [shape_of((count, width), BF)], 2, nbytes=3 * 2**20, limit=16 * 2**20)(
        pieces, returned
    )[0]
    token_grad = whole(
        token_grad_kernel, [shape_of((count, width), BF)], 2, nbytes=3 * 2**20, limit=16 * 2**20
    )(pick, grad_back)[0]

    down_grad = ring_sum(1, *partials(y, grad_rows, [hid], size))[0]
    gate_grad, up_grad = ring_sum(2, *partials(y, expert_rows, [grad_gate, grad_up], size))
    return (output, token_grad, gate_grad, up_grad, down_grad)


def solution(mesh):
    both = ("dp", "expert")
    return jax.shard_map(
        shards,
        mesh=mesh,
        in_specs=(
            P(both, None),
            P(both, None),
            P(both, None),
            P(both),
            P(),
            P("expert", "dp", None),
            P("expert", "dp", None),
            P("expert", "dp", None),
            P(both, None),
        ),
        out_specs=(
            P(both, None),
            P(both, None),
            P("expert", "dp", None),
            P("expert", "dp", None),
            P("expert", "dp", None),
        ),
        check_vma=False,
    )
```

```python
import functools

import jax
import jax.numpy as jnp
from jax import lax
from jax.experimental import pallas as pl
from jax.experimental.pallas import tpu as pltpu
from jax.sharding import PartitionSpec as P


BF = jnp.bfloat16
F32 = jnp.float32
FIRST = (((0,), (0,)), ((), ()))
LAST = (((1,), (1,)), ((), ()))
VMEM = pl.BlockSpec(memory_space=pltpu.VMEM)
SMEM = pl.BlockSpec(memory_space=pltpu.SMEM)
LIMIT = 67_043_328


def shape_of(shape, dtype):
    return jax.ShapeDtypeStruct(shape, dtype)


def whole(kernel, outs, n_in, flops=0, nbytes=0, smem=(), limit=LIMIT):
    call = pl.pallas_call(
        kernel,
        out_shape=outs,
        in_specs=[SMEM if i in smem else VMEM for i in range(n_in)],
        out_specs=[VMEM for _ in outs],
        compiler_params=pltpu.CompilerParams(vmem_limit_bytes=limit),
        cost_estimate=pl.CostEstimate(flops=flops, bytes_accessed=nbytes, transcendentals=0),
    )
    return call


def chosen(place, slots):
    spots = lax.broadcasted_iota(jnp.int32, (slots, place.shape[1]), 0)
    return [place[k : k + 1, :] == spots for k in range(place.shape[0])]


def added(terms):
    total = terms[0]
    for term in terms[1:]:
        total = total + term
    return total


def send_kernel(
    members,
    capacity,
    bucket_ref,
    table_ref,
    ids_ref,
    level_ref,
    tokens_ref,
    grad_ref,
    rows_ref,
    place_ref,
    gate_ref,
):
    top, count = ids_ref.shape
    width = tokens_ref.shape[1]
    names = lax.broadcasted_iota(jnp.int32, (members, count), 0)
    before = (
        lax.broadcasted_iota(jnp.int32, (count, count), 0)
        < lax.broadcasted_iota(jnp.int32, (count, count), 1)
    ).astype(BF)
    ahead = jnp.zeros((members, 1), F32)
    places = []
    for k in range(top):
        ids = ids_ref[k : k + 1, :]
        hot = (ids == names).astype(F32)
        earlier = jnp.dot(hot.astype(BF), before, preferred_element_type=F32) + ahead
        rank = jnp.sum(hot * earlier, axis=0, keepdims=True).astype(jnp.int32)
        ahead = ahead + jnp.sum(hot, axis=1, keepdims=True)
        places.append(ids * capacity + rank)
        place_ref[k : k + 1, :] = places[-1]
    trajs = bucket_ref.shape[0]
    level = level_ref[...]
    traj = lax.broadcasted_iota(jnp.int32, (top, count), 1) // (count // trajs)
    gate = jnp.zeros((top, count), F32)
    for at in range(table_ref.shape[1]):
        entry = jnp.zeros((top, count), F32)
        for j in range(trajs):
            entry = jnp.where(traj == j, table_ref[bucket_ref[j], at], entry)
        gate = jnp.where(level == at, entry, gate)
    gate_ref[...] = gate
    spots = lax.broadcasted_iota(jnp.int32, (members * capacity, count), 0)
    hots = [place == spots for place in places]
    pick = added([hot.astype(F32) for hot in hots]).astype(BF)
    rows_ref[:, :width] = jnp.dot(pick, tokens_ref[...], preferred_element_type=F32).astype(BF)
    gated = added([jnp.where(hot, gate[k : k + 1, :], 0.0) for k, hot in enumerate(hots)])
    slot_gate = jnp.sum(gated, axis=1, keepdims=True)
    grads = jnp.dot(pick, grad_ref[...], preferred_element_type=F32)
    rows_ref[:, width:] = (grads * slot_gate).astype(BF)


def pick_kernel(place_ref, gate_ref, pick_ref, gated_ref):
    hots = chosen(place_ref[...], pick_ref.shape[1])
    pick_ref[...] = added([hot.astype(F32) for hot in hots]).T.astype(BF)
    gate = gate_ref[...]
    gated_ref[...] = added(
        [jnp.where(hot, gate[k : k + 1, :], 0.0) for k, hot in enumerate(hots)]
    ).T


def split_kernel(gated_ref, pieces_ref):
    rest = gated_ref[...]
    for i in range(pieces_ref.shape[0]):
        piece = rest.astype(BF)
        pieces_ref[i] = piece
        rest = rest - piece.astype(F32)


def columns(offset, size):
    return pl.ds(pl.multiple_of(offset, 128), size)


def offsets(y, n, size):
    at = lambda j: lax.rem(y + j, n) * size
    half = size // 2
    return [(at(0), size), (at(3), size), (at(1), size), (at(2), half), (at(2) + half, half)]


def middle_kernel(
    tile,
    y_ref,
    rows_hbm,
    gate_w,
    up_w,
    down_w,
    below,
    above,
    far_a,
    far_b,
    back_hbm,
    hid_hbm,
    gg_hbm,
    gu_hbm,
    rows,
    w_gate,
    w_up,
    w_down,
    back,
    hid,
    gg,
    gu,
    row_sem,
    weight_sem,
    act_sem,
    back_sem,
):
    hidden = hid.shape[1]
    width = rows.shape[1] // 2
    spots = offsets(y_ref[0], 4, width // 4)

    def fetch_rows(part):
        at = slice(part * width, (part + 1) * width)
        copy = pltpu.make_async_copy(rows_hbm.at[:, at], rows.at[:, at], row_sem.at[part])
        copy.start()
        return [copy]

    def fetch_weight(i, shard, held):
        sources = [shard.at[0]] + [ref.at[i] for ref in (below, above, far_a, far_b)]
        copies = [
            pltpu.make_async_copy(
                source, held.at[pl.ds(pl.multiple_of(off, 256), size), :], weight_sem.at[i, j]
            )
            for j, (source, (off, size)) in enumerate(zip(sources, spots))
        ]
        for copy in copies:
            copy.start()
        return copies

    waits = [
        fetch_rows(0) + fetch_weight(0, gate_w, w_gate),
        fetch_weight(1, up_w, w_up),
        fetch_rows(1) + fetch_weight(2, down_w, w_down),
    ]
    tiles = [slice(at, at + tile) for at in range(0, hidden, tile)]

    def into(i, base, held, at):
        if at.start == 0:
            for copy in waits[i]:
                copy.wait()
        return jnp.dot(rows[:, base : base + width], held[:, at], preferred_element_type=F32)

    for at in tiles:
        gate_act = into(0, 0, w_gate, at)
        up_act = into(1, 0, w_up, at)
        grad = into(2, width, w_down, at)
        s = jax.nn.sigmoid(gate_act)
        swish = gate_act * s
        hid[:, at] = (swish * up_act).astype(BF)
        gg[:, at] = (grad * up_act * s * (1.0 + gate_act * (1.0 - s))).astype(BF)
        gu[:, at] = (grad * swish).astype(BF)
    puts = []
    for i, (held, out) in enumerate(((hid, hid_hbm), (gg, gg_hbm), (gu, gu_hbm))):
        puts.append(pltpu.make_async_copy(held, out, act_sem.at[i]))
        puts[-1].start()

    def outof(act, held, at):
        return lax.dot_general(act[...], held[at, :], LAST, preferred_element_type=F32)

    count = back_sem.shape[0]
    span = 2 * width // count
    for c in range(count):
        at = slice(c * span, (c + 1) * span)
        if at.start < width:
            part = outof(hid, w_down, at)
        else:
            inner = slice(at.start - width, at.stop - width)
            part = outof(gg, w_gate, inner) + outof(gu, w_up, inner)
        back[:, at] = part.astype(BF)
        puts.append(pltpu.make_async_copy(back.at[:, at], back_hbm.at[:, at], back_sem.at[c]))
        puts[-1].start()
    for put in puts:
        put.wait()


def partial_kernel(parts, base, y_ref, rows_ref, *refs):
    acts, (own_ref, up_ref, dn_ref, up_a, dn_b) = refs[:parts], refs[parts:]
    size = own_ref.shape[0]
    half = size // 2
    y = y_ref[0]
    spots = [(2, 0, up_ref, 0, half), (1, half, up_ref, half, half)]
    spots += [(2, half, dn_ref, 0, half), (3, 0, dn_ref, half, half)]
    spots += [(1, 0, up_a, 0, half), (3, half, dn_b, 0, half), (0, 0, own_ref, 0, size)]
    for j, lead, ref, top, length in spots:
        rows = rows_ref[:, columns(base + lax.rem(y + j, 4) * size + lead, length)]
        at = 0
        for a in acts:
            ref[top : top + length, at : at + a.shape[1]] = lax.dot_general(
                rows, a[...], FIRST, preferred_element_type=F32
            ).astype(BF)
            at += a.shape[1]


def partials(y, rows, base, acts, size):
    wide = sum(a.shape[1] for a in acts)
    full, half = shape_of((size, wide), BF), shape_of((size // 2, wide), BF)
    return whole(
        functools.partial(partial_kernel, len(acts), base),
        [full, full, full, half, half],
        2 + len(acts),
        flops=rows.size * wide,
        nbytes=2 * (rows.size + 4 * size * wide),
        smem=(0,),
        limit=24 * 2**20,
    )(y, rows, *acts)


def sum_kernel(own_ref, up_ref, dn_ref, below_ref, above_ref, *outs):
    half = below_ref.shape[0]
    hidden = outs[0].shape[2]
    for i, out in enumerate(outs):
        at = slice(i * hidden, (i + 1) * hidden)
        out[0, :half] = (
            own_ref[:half, at].astype(F32)
            + below_ref[:, at].astype(F32)
            + dn_ref[half:, at].astype(F32)
        )
        out[0, half:] = (
            own_ref[half:, at].astype(F32)
            + up_ref[half:, at].astype(F32)
            + above_ref[:, at].astype(F32)
        )


def combine_kernel(pieces_ref, pick_ref, rows_ref, out_ref, grad_ref):
    width = out_ref.shape[1]
    rows = rows_ref[:, :width]
    out_ref[...] = added(
        [
            jnp.dot(pieces_ref[i], rows, preferred_element_type=F32)
            for i in range(pieces_ref.shape[0])
        ]
    ).astype(BF)
    grad_ref[...] = jnp.dot(
        pick_ref[...], rows_ref[:, width:], preferred_element_type=F32
    ).astype(BF)


def move_rows(rows, members):
    depth, width = rows.shape
    buffer = rows.reshape(members, depth // members, width)
    moved = lax.all_to_all(buffer, "expert", split_axis=0, concat_axis=0, tiled=True)
    return moved.reshape(depth, width)


def shift(x, by):
    return lax.ppermute(x, "dp", [(i, (i + by) % 4) for i in range(4)])


def ring_gather(weights):
    shard = jnp.concatenate(weights, axis=0)
    half = shard.shape[1] // 2
    below, above = shift(shard, 1), shift(shard, -1)
    far_a = shift(below[:, :half], 1)
    far_b = shift(above[:, half:], -1)
    return below, above, far_a, far_b


def ring_sum(parts, own, up, dn, up_a, dn_b):
    size, wide = own.shape
    half = size // 2
    got_up, got_dn = shift(up, 1), shift(dn, -1)
    up_a = (up_a.astype(F32) + got_up[:half].astype(F32)).astype(BF)
    dn_b = (dn_b.astype(F32) + got_dn[:half].astype(F32)).astype(BF)
    below, above = shift(up_a, 1), shift(dn_b, -1)
    return whole(
        sum_kernel,
        [shape_of((1, size, wide // parts), F32)] * parts,
        5,
        nbytes=12 * size * wide,
        limit=24 * 2**20,
    )(own, got_up, got_dn, below, above)


def shards(
    tokens,
    expert_ids,
    gate_level,
    cost_bucket,
    gate_table,
    gate_weight,
    up_weight,
    down_weight,
    out_grad,
):
    count, width = tokens.shape
    top = expert_ids.shape[1]
    members = lax.axis_size("expert")
    capacity = min(count, 4 * count * top // (3 * members))
    slots = members * capacity
    size, hidden = gate_weight.shape[1:]
    y = lax.axis_index("dp").astype(jnp.int32).reshape(1)

    rows, place, gates = whole(
        functools.partial(send_kernel, members, capacity),
        [
            shape_of((slots, 2 * width), BF),
            shape_of((top, count), jnp.int32),
            shape_of((top, count), F32),
        ],
        6,
        nbytes=6 * 2**20,
        smem=(0, 1),
    )(cost_bucket, gate_table, expert_ids.T, gate_level.T, tokens, out_grad)
    moved = move_rows(rows, members)
    pick, gated = whole(
        pick_kernel,
        [shape_of((count, slots), BF), shape_of((count, slots), F32)],
        2,
        nbytes=2**20,
        limit=16 * 2**20,
    )(place, gates)
    pieces = whole(
        split_kernel, [shape_of((2, count, slots), BF)], 1, nbytes=2**20, limit=16 * 2**20
    )(gated)[0]

    weights = [gate_weight, up_weight, down_weight]
    act = shape_of((slots, hidden), BF)
    any_space = pl.BlockSpec(memory_space=pl.ANY)
    dma = pltpu.SemaphoreType.DMA
    back, hid, grad_gate, grad_up = pl.pallas_call(
        functools.partial(middle_kernel, 256),
        out_shape=[shape_of((slots, 2 * width), BF), act, act, act],
        in_specs=[SMEM] + [any_space] * 8,
        out_specs=[any_space] * 4,
        scratch_shapes=[pltpu.VMEM((slots, 2 * width), BF)]
        + [pltpu.VMEM((width, hidden), BF)] * 3
        + [pltpu.VMEM((slots, 2 * width), BF)]
        + [pltpu.VMEM((slots, hidden), BF)] * 3
        + [dma((2,)), dma((3, 5)), dma((3,)), dma((8,))],
        compiler_params=pltpu.CompilerParams(vmem_limit_bytes=LIMIT),
        cost_estimate=pl.CostEstimate(
            flops=12 * slots * width * hidden, bytes_accessed=20 * 2**20, transcendentals=0
        ),
        name="middle",
    )(y, moved, *weights, *ring_gather(weights))
    returned = move_rows(back, members)

    down_grad = ring_sum(1, *partials(y, moved, width, [hid], size))[0]
    gate_grad, up_grad = ring_sum(2, *partials(y, moved, 0, [grad_gate, grad_up], size))
    output, token_grad = whole(
        combine_kernel, [shape_of((count, width), BF)] * 2, 3, nbytes=6 * 2**20, limit=16 * 2**20
    )(pieces, pick, returned)
    return (output, token_grad, gate_grad, up_grad, down_grad)


def solution(mesh):
    both = ("dp", "expert")
    return jax.shard_map(
        shards,
        mesh=mesh,
        in_specs=(
            P(both, None),
            P(both, None),
            P(both, None),
            P(both),
            P(),
            P("expert", "dp", None),
            P("expert", "dp", None),
            P("expert", "dp", None),
            P(both, None),
        ),
        out_specs=(
            P(both, None),
            P(both, None),
            P("expert", "dp", None),
            P("expert", "dp", None),
            P("expert", "dp", None),
        ),
        check_vma=False,
    )
```

```python
import functools

import jax
import jax.numpy as jnp
from jax import lax
from jax.experimental import pallas as pl
from jax.experimental.pallas import tpu as pltpu
from jax.sharding import PartitionSpec as P


BF = jnp.bfloat16
F32 = jnp.float32
FIRST = (((0,), (0,)), ((), ()))
LAST = (((1,), (1,)), ((), ()))
VMEM = pl.BlockSpec(memory_space=pltpu.VMEM)
SMEM = pl.BlockSpec(memory_space=pltpu.SMEM)
LIMIT = 67_043_328


def shape_of(shape, dtype):
    return jax.ShapeDtypeStruct(shape, dtype)


def whole(kernel, outs, n_in, flops=0, nbytes=0, smem=(), limit=LIMIT):
    call = pl.pallas_call(
        kernel,
        out_shape=outs,
        in_specs=[SMEM if i in smem else VMEM for i in range(n_in)],
        out_specs=[VMEM for _ in outs],
        compiler_params=pltpu.CompilerParams(vmem_limit_bytes=limit),
        cost_estimate=pl.CostEstimate(flops=flops, bytes_accessed=nbytes, transcendentals=0),
    )
    return call


def chosen(place, slots):
    spots = lax.broadcasted_iota(jnp.int32, (slots, place.shape[1]), 0)
    return [place[k : k + 1, :] == spots for k in range(place.shape[0])]


def added(terms):
    total = terms[0]
    for term in terms[1:]:
        total = total + term
    return total


def send_kernel(
    members,
    capacity,
    bucket_ref,
    table_ref,
    ids_ref,
    level_ref,
    tokens_ref,
    grad_ref,
    rows_ref,
    place_ref,
    gate_ref,
):
    top, count = ids_ref.shape
    width = tokens_ref.shape[1]
    names = lax.broadcasted_iota(jnp.int32, (members, count), 0)
    before = (
        lax.broadcasted_iota(jnp.int32, (count, count), 0)
        < lax.broadcasted_iota(jnp.int32, (count, count), 1)
    ).astype(BF)
    ahead = jnp.zeros((members, 1), F32)
    places = []
    for k in range(top):
        ids = ids_ref[k : k + 1, :]
        hot = (ids == names).astype(F32)
        earlier = jnp.dot(hot.astype(BF), before, preferred_element_type=F32) + ahead
        rank = jnp.sum(hot * earlier, axis=0, keepdims=True).astype(jnp.int32)
        ahead = ahead + jnp.sum(hot, axis=1, keepdims=True)
        places.append(ids * capacity + rank)
        place_ref[k : k + 1, :] = places[-1]
    trajs = bucket_ref.shape[0]
    level = level_ref[...]
    traj = lax.broadcasted_iota(jnp.int32, (top, count), 1) // (count // trajs)
    gate = jnp.zeros((top, count), F32)
    for at in range(table_ref.shape[1]):
        entry = jnp.zeros((top, count), F32)
        for j in range(trajs):
            entry = jnp.where(traj == j, table_ref[bucket_ref[j], at], entry)
        gate = jnp.where(level == at, entry, gate)
    gate_ref[...] = gate
    spots = lax.broadcasted_iota(jnp.int32, (members * capacity, count), 0)
    hots = [place == spots for place in places]
    pick = added([hot.astype(F32) for hot in hots]).astype(BF)
    rows_ref[:, :width] = jnp.dot(pick, tokens_ref[...], preferred_element_type=F32).astype(BF)
    gated = added([jnp.where(hot, gate[k : k + 1, :], 0.0) for k, hot in enumerate(hots)])
    slot_gate = jnp.sum(gated, axis=1, keepdims=True)
    grads = jnp.dot(pick, grad_ref[...], preferred_element_type=F32)
    rows_ref[:, width:] = (grads * slot_gate).astype(BF)


def pick_kernel(place_ref, gate_ref, pick_ref, gated_ref):
    hots = chosen(place_ref[...], pick_ref.shape[1])
    pick_ref[...] = added([hot.astype(F32) for hot in hots]).T.astype(BF)
    gate = gate_ref[...]
    gated_ref[...] = added(
        [jnp.where(hot, gate[k : k + 1, :], 0.0) for k, hot in enumerate(hots)]
    ).T


def split_kernel(gated_ref, pieces_ref):
    rest = gated_ref[...]
    count = rest.shape[0]
    for at in range(0, pieces_ref.shape[0], count):
        piece = rest.astype(BF)
        pieces_ref[at : at + count] = piece
        rest = rest - piece.astype(F32)


def columns(offset, size):
    return pl.ds(pl.multiple_of(offset, 128), size)


def offsets(y, n, size):
    at = lambda j: lax.rem(y + j, n) * size
    half = size // 2
    return [(at(0), size), (at(3), size), (at(1), size), (at(2), half), (at(2) + half, half)]


def middle_kernel(
    tile,
    y_ref,
    rows_hbm,
    gate_w,
    up_w,
    down_w,
    below,
    above,
    far_a,
    far_b,
    back_hbm,
    hid_hbm,
    gg_hbm,
    gu_hbm,
    rows,
    w_gate,
    w_up,
    w_down,
    back,
    hid,
    gg,
    gu,
    gate_out,
    up_out,
    row_sem,
    weight_sem,
    act_sem,
    back_sem,
):
    hidden = hid.shape[1]
    width = rows.shape[1] // 2
    quarter = width // 4
    spots = offsets(y_ref[0], 4, quarter)
    tiles = [slice(at, at + tile) for at in range(0, hidden, tile)]

    def begin(source, held, sem):
        copy = pltpu.make_async_copy(source, held, sem)
        copy.start()
        return copy

    def fetch_weight(i, shard, held, chosen_pieces):
        sources = [shard.at[0]] + [ref.at[i] for ref in (below, above, far_a, far_b)]
        return [
            begin(
                sources[j],
                held.at[pl.ds(pl.multiple_of(spots[j][0], 256), spots[j][1]), :],
                weight_sem.at[i, j],
            )
            for j in chosen_pieces
        ]

    chunks = [(0,), (1,), (2,), (3, 4)]
    arrivals = []
    for c, chunk in enumerate(chunks):
        at = columns(spots[chunk[0]][0], quarter)
        arrivals.append(
            [begin(rows_hbm.at[:, at], rows.at[:, at], row_sem.at[c])]
            + fetch_weight(0, gate_w, w_gate, chunk)
            + fetch_weight(1, up_w, w_up, chunk)
        )
    late = [
        begin(rows_hbm.at[:, width:], rows.at[:, width:], row_sem.at[len(chunks)])
    ] + fetch_weight(2, down_w, w_down, range(5))

    for c, chunk in enumerate(chunks):
        for copy in arrivals[c]:
            copy.wait()
        off = spots[chunk[0]][0]
        some = rows[:, columns(off, quarter)]
        for held, out in ((w_gate, gate_out), (w_up, up_out)):
            for at in tiles:
                part = jnp.dot(
                    some,
                    held[pl.ds(pl.multiple_of(off, 512), quarter), at],
                    preferred_element_type=F32,
                )
                out[:, at] = part if c == 0 else out[:, at] + part
    for copy in late:
        copy.wait()
    for at in tiles:
        grad = jnp.dot(rows[:, width:], w_down[:, at], preferred_element_type=F32)
        gate_act, up_act = gate_out[:, at], up_out[:, at]
        s = jax.nn.sigmoid(gate_act)
        swish = gate_act * s
        hid[:, at] = (swish * up_act).astype(BF)
        gg[:, at] = (grad * up_act * s * (1.0 + gate_act * (1.0 - s))).astype(BF)
        gu[:, at] = (grad * swish).astype(BF)
    puts = []
    for i, (held, out) in enumerate(((hid, hid_hbm), (gg, gg_hbm), (gu, gu_hbm))):
        puts.append(pltpu.make_async_copy(held, out, act_sem.at[i]))
        puts[-1].start()

    def outof(act, held, at):
        return lax.dot_general(act[...], held[at, :], LAST, preferred_element_type=F32)

    count = back_sem.shape[0]
    span = 2 * width // count
    for c in range(count):
        at = slice(c * span, (c + 1) * span)
        if at.start < width:
            part = outof(hid, w_down, at)
        else:
            inner = slice(at.start - width, at.stop - width)
            part = outof(gg, w_gate, inner) + outof(gu, w_up, inner)
        back[:, at] = part.astype(BF)
        puts.append(pltpu.make_async_copy(back.at[:, at], back_hbm.at[:, at], back_sem.at[c]))
        puts[-1].start()
    for put in puts:
        put.wait()


def partial_kernel(parts, base, y_ref, rows_ref, *refs):
    acts, (own_ref, up_ref, dn_ref, up_a, dn_b) = refs[:parts], refs[parts:]
    size = own_ref.shape[0]
    half = size // 2
    y = y_ref[0]
    spots = [(2, 0, up_ref, 0, half), (1, half, up_ref, half, half)]
    spots += [(2, half, dn_ref, 0, half), (3, 0, dn_ref, half, half)]
    spots += [(1, 0, up_a, 0, half), (3, half, dn_b, 0, half), (0, 0, own_ref, 0, size)]
    for j, lead, ref, top, length in spots:
        rows = rows_ref[:, columns(base + lax.rem(y + j, 4) * size + lead, length)]
        at = 0
        for a in acts:
            ref[top : top + length, at : at + a.shape[1]] = lax.dot_general(
                rows, a[...], FIRST, preferred_element_type=F32
            ).astype(BF)
            at += a.shape[1]


def partials(y, rows, base, acts, size):
    wide = sum(a.shape[1] for a in acts)
    full, half = shape_of((size, wide), BF), shape_of((size // 2, wide), BF)
    return whole(
        functools.partial(partial_kernel, len(acts), base),
        [full, full, full, half, half],
        2 + len(acts),
        flops=rows.size * wide,
        nbytes=2 * (rows.size + 4 * size * wide),
        smem=(0,),
        limit=24 * 2**20,
    )(y, rows, *acts)


def sum_kernel(own_ref, up_ref, dn_ref, below_ref, above_ref, *outs):
    half = below_ref.shape[0]
    hidden = outs[0].shape[2]
    for i, out in enumerate(outs):
        at = slice(i * hidden, (i + 1) * hidden)
        out[0, :half] = (
            own_ref[:half, at].astype(F32)
            + below_ref[:, at].astype(F32)
            + dn_ref[half:, at].astype(F32)
        )
        out[0, half:] = (
            own_ref[half:, at].astype(F32)
            + up_ref[half:, at].astype(F32)
            + above_ref[:, at].astype(F32)
        )


def combine_kernel(pieces_ref, pick_ref, rows_ref, out_ref, grad_ref):
    count, width = out_ref.shape
    parts = jnp.dot(pieces_ref[...], rows_ref[:, :width], preferred_element_type=F32)
    out_ref[...] = added(
        [parts[at : at + count] for at in range(0, parts.shape[0], count)]
    ).astype(BF)
    grad_ref[...] = jnp.dot(
        pick_ref[...], rows_ref[:, width:], preferred_element_type=F32
    ).astype(BF)


def move_rows(rows, members):
    depth, width = rows.shape
    buffer = rows.reshape(members, depth // members, width)
    moved = lax.all_to_all(buffer, "expert", split_axis=0, concat_axis=0, tiled=True)
    return moved.reshape(depth, width)


def shift(x, by):
    return lax.ppermute(x, "dp", [(i, (i + by) % 4) for i in range(4)])


def ring_gather(weights):
    shard = jnp.concatenate(weights, axis=0)
    half = shard.shape[1] // 2
    below, above = shift(shard, 1), shift(shard, -1)
    far_a = shift(below[:, :half], 1)
    far_b = shift(above[:, half:], -1)
    return below, above, far_a, far_b


def ring_sum(parts, own, up, dn, up_a, dn_b):
    size, wide = own.shape
    half = size // 2
    got_up, got_dn = shift(up, 1), shift(dn, -1)
    up_a = (up_a.astype(F32) + got_up[:half].astype(F32)).astype(BF)
    dn_b = (dn_b.astype(F32) + got_dn[:half].astype(F32)).astype(BF)
    below, above = shift(up_a, 1), shift(dn_b, -1)
    return whole(
        sum_kernel,
        [shape_of((1, size, wide // parts), F32)] * parts,
        5,
        nbytes=12 * size * wide,
        limit=24 * 2**20,
    )(own, got_up, got_dn, below, above)


def shards(
    tokens,
    expert_ids,
    gate_level,
    cost_bucket,
    gate_table,
    gate_weight,
    up_weight,
    down_weight,
    out_grad,
):
    count, width = tokens.shape
    top = expert_ids.shape[1]
    members = lax.axis_size("expert")
    capacity = min(count, 4 * count * top // (3 * members))
    slots = members * capacity
    size, hidden = gate_weight.shape[1:]
    y = lax.axis_index("dp").astype(jnp.int32).reshape(1)

    rows, place, gates = whole(
        functools.partial(send_kernel, members, capacity),
        [
            shape_of((slots, 2 * width), BF),
            shape_of((top, count), jnp.int32),
            shape_of((top, count), F32),
        ],
        6,
        nbytes=6 * 2**20,
        smem=(0, 1),
    )(cost_bucket, gate_table, expert_ids.T, gate_level.T, tokens, out_grad)
    moved = move_rows(rows, members)
    pick, gated = whole(
        pick_kernel,
        [shape_of((count, slots), BF), shape_of((count, slots), F32)],
        2,
        nbytes=2**20,
        limit=16 * 2**20,
    )(place, gates)
    pieces = whole(
        split_kernel,
        [shape_of((2 * count, slots), BF)],
        1,
        nbytes=2**20,
        limit=16 * 2**20,
    )(gated)[0]

    weights = [gate_weight, up_weight, down_weight]
    act = shape_of((slots, hidden), BF)
    any_space = pl.BlockSpec(memory_space=pl.ANY)
    dma = pltpu.SemaphoreType.DMA
    back, hid, grad_gate, grad_up = pl.pallas_call(
        functools.partial(middle_kernel, 256),
        out_shape=[shape_of((slots, 2 * width), BF), act, act, act],
        in_specs=[SMEM] + [any_space] * 8,
        out_specs=[any_space] * 4,
        scratch_shapes=[pltpu.VMEM((slots, 2 * width), BF)]
        + [pltpu.VMEM((width, hidden), BF)] * 3
        + [pltpu.VMEM((slots, 2 * width), BF)]
        + [pltpu.VMEM((slots, hidden), BF)] * 3
        + [pltpu.VMEM((slots, hidden), F32)] * 2
        + [dma((5,)), dma((3, 5)), dma((3,)), dma((16,))],
        compiler_params=pltpu.CompilerParams(vmem_limit_bytes=LIMIT),
        cost_estimate=pl.CostEstimate(
            flops=12 * slots * width * hidden, bytes_accessed=20 * 2**20, transcendentals=0
        ),
        name="middle",
    )(y, moved, *weights, *ring_gather(weights))
    returned = move_rows(back, members)

    down_grad = ring_sum(1, *partials(y, moved, width, [hid], size))[0]
    gate_grad, up_grad = ring_sum(2, *partials(y, moved, 0, [grad_gate, grad_up], size))
    output, token_grad = whole(
        combine_kernel,
        [shape_of((count, width), BF)] * 2,
        3,
        nbytes=6 * 2**20,
        limit=16 * 2**20,
    )(pieces, pick, returned)
    return (output, token_grad, gate_grad, up_grad, down_grad)


def solution(mesh):
    both = ("dp", "expert")
    return jax.shard_map(
        shards,
        mesh=mesh,
        in_specs=(
            P(both, None),
            P(both, None),
            P(both, None),
            P(both),
            P(),
            P("expert", "dp", None),
            P("expert", "dp", None),
            P("expert", "dp", None),
            P(both, None),
        ),
        out_specs=(
            P(both, None),
            P(both, None),
            P("expert", "dp", None),
            P("expert", "dp", None),
            P("expert", "dp", None),
        ),
        check_vma=False,
    )
```

```python
import functools

import jax
import jax.numpy as jnp
from jax import lax
from jax.experimental import pallas as pl
from jax.experimental.pallas import tpu as pltpu
from jax.sharding import PartitionSpec as P


BF = jnp.bfloat16
F32 = jnp.float32
FIRST = (((0,), (0,)), ((), ()))
LAST = (((1,), (1,)), ((), ()))
VMEM = pl.BlockSpec(memory_space=pltpu.VMEM)
SMEM = pl.BlockSpec(memory_space=pltpu.SMEM)
LIMIT = 67_043_328


def shape_of(shape, dtype):
    return jax.ShapeDtypeStruct(shape, dtype)


def whole(kernel, outs, n_in, flops=0, nbytes=0, smem=(), limit=LIMIT):
    call = pl.pallas_call(
        kernel,
        out_shape=outs,
        in_specs=[SMEM if i in smem else VMEM for i in range(n_in)],
        out_specs=[VMEM for _ in outs],
        compiler_params=pltpu.CompilerParams(vmem_limit_bytes=limit),
        cost_estimate=pl.CostEstimate(flops=flops, bytes_accessed=nbytes, transcendentals=0),
    )
    return call


def chosen(place, slots):
    spots = lax.broadcasted_iota(jnp.int32, (slots, place.shape[1]), 0)
    return [place[k : k + 1, :] == spots for k in range(place.shape[0])]


def added(terms):
    total = terms[0]
    for term in terms[1:]:
        total = total + term
    return total


def send_kernel(
    members,
    capacity,
    bucket_ref,
    table_ref,
    ids_ref,
    level_ref,
    tokens_ref,
    grad_ref,
    rows_ref,
    place_ref,
    gate_ref,
):
    top, count = ids_ref.shape
    width = tokens_ref.shape[1]
    names = lax.broadcasted_iota(jnp.int32, (members, count), 0)
    before = (
        lax.broadcasted_iota(jnp.int32, (count, count), 0)
        < lax.broadcasted_iota(jnp.int32, (count, count), 1)
    ).astype(BF)
    ahead = jnp.zeros((members, 1), F32)
    places = []
    for k in range(top):
        ids = ids_ref[k : k + 1, :]
        hot = (ids == names).astype(F32)
        earlier = jnp.dot(hot.astype(BF), before, preferred_element_type=F32) + ahead
        rank = jnp.sum(hot * earlier, axis=0, keepdims=True).astype(jnp.int32)
        ahead = ahead + jnp.sum(hot, axis=1, keepdims=True)
        places.append(ids * capacity + rank)
        place_ref[k : k + 1, :] = places[-1]
    trajs = bucket_ref.shape[0]
    level = level_ref[...]
    traj = lax.broadcasted_iota(jnp.int32, (top, count), 1) // (count // trajs)
    gate = jnp.zeros((top, count), F32)
    for at in range(table_ref.shape[1]):
        entry = jnp.zeros((top, count), F32)
        for j in range(trajs):
            entry = jnp.where(traj == j, table_ref[bucket_ref[j], at], entry)
        gate = jnp.where(level == at, entry, gate)
    gate_ref[...] = gate
    spots = lax.broadcasted_iota(jnp.int32, (members * capacity, count), 0)
    hots = [place == spots for place in places]
    pick = added([hot.astype(F32) for hot in hots]).astype(BF)
    rows_ref[:, :width] = jnp.dot(pick, tokens_ref[...], preferred_element_type=F32).astype(BF)
    gated = added([jnp.where(hot, gate[k : k + 1, :], 0.0) for k, hot in enumerate(hots)])
    slot_gate = jnp.sum(gated, axis=1, keepdims=True)
    grads = jnp.dot(pick, grad_ref[...], preferred_element_type=F32)
    rows_ref[:, width:] = (grads * slot_gate).astype(BF)


def pick_kernel(place_ref, gate_ref, pick_ref, gated_ref):
    hots = chosen(place_ref[...], pick_ref.shape[1])
    pick_ref[...] = added([hot.astype(F32) for hot in hots]).T.astype(BF)
    gate = gate_ref[...]
    gated_ref[...] = added(
        [jnp.where(hot, gate[k : k + 1, :], 0.0) for k, hot in enumerate(hots)]
    ).T


def split_kernel(gated_ref, pieces_ref):
    rest = gated_ref[...]
    count = rest.shape[0]
    for at in range(0, pieces_ref.shape[0], count):
        piece = rest.astype(BF)
        pieces_ref[at : at + count] = piece
        rest = rest - piece.astype(F32)


def columns(offset, size):
    return pl.ds(pl.multiple_of(offset, 128), size)


def offsets(y, n, size):
    at = lambda j: lax.rem(y + j, n) * size
    half = size // 2
    return [(at(0), size), (at(3), size), (at(1), size), (at(2), half), (at(2) + half, half)]


def middle_kernel(
    tile,
    y_ref,
    rows_hbm,
    gate_w,
    up_w,
    down_w,
    below,
    above,
    far_a,
    far_b,
    back_hbm,
    hid_hbm,
    gg_hbm,
    gu_hbm,
    rows,
    w_gate,
    w_up,
    w_down,
    back,
    hid,
    gg,
    gu,
    gate_out,
    up_out,
    row_sem,
    weight_sem,
    act_sem,
    back_sem,
):
    hidden = hid.shape[1]
    width = rows.shape[1] // 2
    quarter = width // 4
    spots = offsets(y_ref[0], 4, quarter)
    tiles = [slice(at, at + tile) for at in range(0, hidden, tile)]

    def begin(source, held, sem):
        copy = pltpu.make_async_copy(source, held, sem)
        copy.start()
        return copy

    def fetch_weight(i, shard, held, chosen_pieces):
        sources = [shard.at[0]] + [ref.at[i] for ref in (below, above, far_a, far_b)]
        return [
            begin(
                sources[j],
                held.at[pl.ds(pl.multiple_of(spots[j][0], 256), spots[j][1]), :],
                weight_sem.at[i, j],
            )
            for j in chosen_pieces
        ]

    chunks = [(0,), (1,), (2,), (3, 4)]
    arrivals = []
    for c, chunk in enumerate(chunks):
        at = columns(spots[chunk[0]][0], quarter)
        arrivals.append(
            [begin(rows_hbm.at[:, at], rows.at[:, at], row_sem.at[c])]
            + fetch_weight(0, gate_w, w_gate, chunk)
            + fetch_weight(1, up_w, w_up, chunk)
        )
    late = [
        begin(rows_hbm.at[:, width:], rows.at[:, width:], row_sem.at[len(chunks)])
    ] + fetch_weight(2, down_w, w_down, range(5))

    for c, chunk in enumerate(chunks):
        for copy in arrivals[c]:
            copy.wait()
        off = spots[chunk[0]][0]
        some = rows[:, columns(off, quarter)]
        for held, out in ((w_gate, gate_out), (w_up, up_out)):
            for at in tiles:
                part = jnp.dot(
                    some,
                    held[pl.ds(pl.multiple_of(off, 512), quarter), at],
                    preferred_element_type=F32,
                )
                out[:, at] = part if c == 0 else out[:, at] + part
    for copy in late:
        copy.wait()
    for at in tiles:
        grad = jnp.dot(rows[:, width:], w_down[:, at], preferred_element_type=F32)
        gate_act, up_act = gate_out[:, at], up_out[:, at]
        s = jax.nn.sigmoid(gate_act)
        swish = gate_act * s
        hid[:, at] = (swish * up_act).astype(BF)
        gg[:, at] = (grad * up_act * s * (1.0 + gate_act * (1.0 - s))).astype(BF)
        gu[:, at] = (grad * swish).astype(BF)
    puts = []
    for i, (held, out) in enumerate(((hid, hid_hbm), (gg, gg_hbm), (gu, gu_hbm))):
        puts.append(pltpu.make_async_copy(held, out, act_sem.at[i]))
        puts[-1].start()

    def outof(act, held, at):
        return lax.dot_general(act[...], held[at, :], LAST, preferred_element_type=F32)

    count = back_sem.shape[0]
    span = 2 * width // count
    for c in range(count):
        at = slice(c * span, (c + 1) * span)
        if at.start < width:
            part = outof(hid, w_down, at)
        else:
            inner = slice(at.start - width, at.stop - width)
            part = outof(gg, w_gate, inner) + outof(gu, w_up, inner)
        back[:, at] = part.astype(BF)
        puts.append(pltpu.make_async_copy(back.at[:, at], back_hbm.at[:, at], back_sem.at[c]))
        puts[-1].start()
    for put in puts:
        put.wait()


def partial_kernel(parts, base, y_ref, rows_ref, *refs):
    acts, (own_ref, up_ref, dn_ref, up_a, dn_b) = refs[:parts], refs[parts:]
    size = own_ref.shape[0]
    half = size // 2
    y = y_ref[0]
    spots = [(2, 0, up_ref, 0, half), (1, half, up_ref, half, half)]
    spots += [(2, half, dn_ref, 0, half), (3, 0, dn_ref, half, half)]
    spots += [(1, 0, up_a, 0, half), (3, half, dn_b, 0, half), (0, 0, own_ref, 0, size)]
    for j, lead, ref, top, length in spots:
        rows = rows_ref[:, columns(base + lax.rem(y + j, 4) * size + lead, length)]
        at = 0
        for a in acts:
            ref[top : top + length, at : at + a.shape[1]] = lax.dot_general(
                rows, a[...], FIRST, preferred_element_type=F32
            ).astype(BF)
            at += a.shape[1]


def partials(y, rows, base, acts, size):
    wide = sum(a.shape[1] for a in acts)
    full, half = shape_of((size, wide), BF), shape_of((size // 2, wide), BF)
    return whole(
        functools.partial(partial_kernel, len(acts), base),
        [full, full, full, half, half],
        2 + len(acts),
        flops=rows.size * wide,
        nbytes=2 * (rows.size + 4 * size * wide),
        smem=(0,),
        limit=24 * 2**20,
    )(y, rows, *acts)


def sum_kernel(own_ref, up_ref, dn_ref, below_ref, above_ref, *outs):
    half = below_ref.shape[0]
    hidden = outs[0].shape[2]
    for i, out in enumerate(outs):
        at = slice(i * hidden, (i + 1) * hidden)
        out[0, :half] = (
            own_ref[:half, at].astype(F32)
            + below_ref[:, at].astype(F32)
            + dn_ref[half:, at].astype(F32)
        )
        out[0, half:] = (
            own_ref[half:, at].astype(F32)
            + up_ref[half:, at].astype(F32)
            + above_ref[:, at].astype(F32)
        )


def combine_kernel(
    pieces_ref, pick_ref, rows_hbm, out_hbm, grad_hbm, rows, out, grad, sem, out_sem
):
    count, width = out.shape
    halves = [slice(0, width), slice(width, 2 * width)]
    gets = [
        pltpu.make_async_copy(rows_hbm.at[:, at], rows.at[:, at], sem.at[i])
        for i, at in enumerate(halves)
    ]
    puts = [
        pltpu.make_async_copy(out, out_hbm, out_sem.at[0]),
        pltpu.make_async_copy(grad, grad_hbm, out_sem.at[1]),
    ]
    for get in gets:
        get.start()
    gets[0].wait()
    parts = jnp.dot(pieces_ref[...], rows[:, :width], preferred_element_type=F32)
    out[...] = added(
        [parts[at : at + count] for at in range(0, parts.shape[0], count)]
    ).astype(BF)
    puts[0].start()
    gets[1].wait()
    grad[...] = jnp.dot(pick_ref[...], rows[:, width:], preferred_element_type=F32).astype(BF)
    puts[1].start()
    for put in puts:
        put.wait()


def move_rows(rows, members):
    depth, width = rows.shape
    buffer = rows.reshape(members, depth // members, width)
    moved = lax.all_to_all(buffer, "expert", split_axis=0, concat_axis=0, tiled=True)
    return moved.reshape(depth, width)


def shift(x, by):
    return lax.ppermute(x, "dp", [(i, (i + by) % 4) for i in range(4)])


def ring_gather(weights):
    shard = jnp.concatenate(weights, axis=0)
    half = shard.shape[1] // 2
    below, above = shift(shard, 1), shift(shard, -1)
    far_a = shift(below[:, :half], 1)
    far_b = shift(above[:, half:], -1)
    return below, above, far_a, far_b


def ring_sum(parts, own, up, dn, up_a, dn_b):
    size, wide = own.shape
    half = size // 2
    got_up, got_dn = shift(up, 1), shift(dn, -1)
    up_a = (up_a.astype(F32) + got_up[:half].astype(F32)).astype(BF)
    dn_b = (dn_b.astype(F32) + got_dn[:half].astype(F32)).astype(BF)
    below, above = shift(up_a, 1), shift(dn_b, -1)
    return whole(
        sum_kernel,
        [shape_of((1, size, wide // parts), F32)] * parts,
        5,
        nbytes=12 * size * wide,
        limit=24 * 2**20,
    )(own, got_up, got_dn, below, above)


def shards(
    tokens,
    expert_ids,
    gate_level,
    cost_bucket,
    gate_table,
    gate_weight,
    up_weight,
    down_weight,
    out_grad,
):
    count, width = tokens.shape
    top = expert_ids.shape[1]
    members = lax.axis_size("expert")
    capacity = min(count, 4 * count * top // (3 * members))
    slots = members * capacity
    size, hidden = gate_weight.shape[1:]
    y = lax.axis_index("dp").astype(jnp.int32).reshape(1)

    rows, place, gates = whole(
        functools.partial(send_kernel, members, capacity),
        [
            shape_of((slots, 2 * width), BF),
            shape_of((top, count), jnp.int32),
            shape_of((top, count), F32),
        ],
        6,
        nbytes=6 * 2**20,
        smem=(0, 1),
    )(cost_bucket, gate_table, expert_ids.T, gate_level.T, tokens, out_grad)
    moved = move_rows(rows, members)
    pick, gated = whole(
        pick_kernel,
        [shape_of((count, slots), BF), shape_of((count, slots), F32)],
        2,
        nbytes=2**20,
        limit=16 * 2**20,
    )(place, gates)
    pieces = whole(
        split_kernel, [shape_of((2 * count, slots), BF)], 1, nbytes=2**20, limit=16 * 2**20
    )(gated)[0]

    weights = [gate_weight, up_weight, down_weight]
    act = shape_of((slots, hidden), BF)
    any_space = pl.BlockSpec(memory_space=pl.ANY)
    dma = pltpu.SemaphoreType.DMA
    back, hid, grad_gate, grad_up = pl.pallas_call(
        functools.partial(middle_kernel, 256),
        out_shape=[shape_of((slots, 2 * width), BF), act, act, act],
        in_specs=[SMEM] + [any_space] * 8,
        out_specs=[any_space] * 4,
        scratch_shapes=[pltpu.VMEM((slots, 2 * width), BF)]
        + [pltpu.VMEM((width, hidden), BF)] * 3
        + [pltpu.VMEM((slots, 2 * width), BF)]
        + [pltpu.VMEM((slots, hidden), BF)] * 3
        + [pltpu.VMEM((slots, hidden), F32)] * 2
        + [dma((5,)), dma((3, 5)), dma((3,)), dma((16,))],
        compiler_params=pltpu.CompilerParams(vmem_limit_bytes=LIMIT),
        cost_estimate=pl.CostEstimate(
            flops=12 * slots * width * hidden, bytes_accessed=20 * 2**20, transcendentals=0
        ),
        name="middle",
    )(y, moved, *weights, *ring_gather(weights))
    returned = move_rows(back, members)

    down_grad = ring_sum(1, *partials(y, moved, width, [hid], size))[0]
    gate_grad, up_grad = ring_sum(2, *partials(y, moved, 0, [grad_gate, grad_up], size))
    token_rows = shape_of((count, width), BF)
    output, token_grad = pl.pallas_call(
        combine_kernel,
        out_shape=[token_rows, token_rows],
        in_specs=[VMEM, VMEM, any_space],
        out_specs=[any_space, any_space],
        scratch_shapes=[pltpu.VMEM((slots, 2 * width), BF)]
        + [pltpu.VMEM((count, width), BF)] * 2
        + [dma((2,)), dma((2,))],
        compiler_params=pltpu.CompilerParams(vmem_limit_bytes=16 * 2**20),
        cost_estimate=pl.CostEstimate(flops=0, bytes_accessed=6 * 2**20, transcendentals=0),
        name="combine",
    )(pieces, pick, returned)
    return (output, token_grad, gate_grad, up_grad, down_grad)


def solution(mesh):
    both = ("dp", "expert")
    return jax.shard_map(
        shards,
        mesh=mesh,
        in_specs=(
            P(both, None),
            P(both, None),
            P(both, None),
            P(both),
            P(),
            P("expert", "dp", None),
            P("expert", "dp", None),
            P("expert", "dp", None),
            P(both, None),
        ),
        out_specs=(
            P(both, None),
            P(both, None),
            P("expert", "dp", None),
            P("expert", "dp", None),
            P("expert", "dp", None),
        ),
        check_vma=False,
    )
```
